512 devices in a mesh: dp: 32 (over y_lo, x, core), expert: 16 (over z, y_hi).
Axes of the slice: x: 4, y: 8 (y_hi: 2, y_lo: 4; y = y_hi * 4 + y_lo), z: 8, core: 2. Of those that a mesh axis runs over, the one named last changes fastest.
Arguments:
- tokens: bfloat16 [65536, 2048], P(('dp', 'expert')), may hold values from -24 to 24
- cotangent: bfloat16 [65536, 2048], P(('dp', 'expert')), may hold values from -6 to 6
- route: int32 [65536, 1], P(('dp', 'expert')), may hold values from 0 to 3; in each aligned block of 128 rows (0 to 127, 128 to 255, ...) at most 48 rows name the same one
- prob: bfloat16 [65536], P(('dp', 'expert')), may hold values from 0.049804688 to 1
- w_gate: float32 [16, 2048, 128], P('expert'), may hold values from -0.125 to 0.125
- w_up: float32 [16, 2048, 128], P('expert'), may hold values from -0.125 to 0.125
- w_down: float32 [16, 2048, 128], P('expert'), may hold values from -0.25 to 0.25
Outputs:
- grad_input: bfloat16 [65536, 2048], P(('dp', 'expert'))
- grad_prob: bfloat16 [65536], P(('dp', 'expert'))
- grad_gate: float32 [16, 2048, 128], P('expert', 'dp')
- grad_up: float32 [16, 2048, 128], P('expert', 'dp')
- grad_down: float32 [16, 2048, 128], P('expert', 'dp')
The draws below stay inside these ranges and needn't reach their ends.
Inputs may be any that keep to these rules, and one draw needn't show every extreme that they name: `route`: within each device's aligned block of 128 rows (devices in the order of dp, then expert) each hot expert is named by at most 48 rows, a bound that some block reaches.
All inputs are finite; a program needn't handle non-finite values.
Results may differ from the reference program's by a relative error of at most 0.003.
Values may be sent and summed in bfloat16 or wider, within the bound.
A program may use at most 128 MiB of HBM per device.

```python
import math
import jax
import jax.numpy as jnp
import numpy as np
from jax import lax

D = 2048
FF = 512
HOT = 4
TOK_DEV = 128
FQ = 128
CAP = 48
SHARDS = 16
TOKENS = 65536
N_DP = 32
N_EXPERT = 16


def with_spikes(values, stream_key, source, target, blocks, factor):
    owner, partner = [(jnp.arange(values.shape[dim]) // (values.shape[dim] // blocks)).reshape([-1 if axis == dim else 1 for axis in range(values.ndim)]) for dim in (source, target)]
    chosen = jax.random.permutation(stream_key, blocks)[partner]
    strong = (owner == chosen) | (owner == (partner + blocks // 2) % blocks)
    return jnp.where(strong, factor * values, values)


def block_levels(rng, dims, split, low, high):
    def one(axis_at, parts):
        steps = jax.random.uniform(jax.random.fold_in(jax.random.fold_in(rng, 6), axis_at), (parts,), jnp.float32, low / len(split), high / len(split))
        return jnp.repeat(jnp.exp(steps), dims[axis_at] // parts).reshape((-1,) + (1,) * (len(dims) - axis_at - 1))

    level = one(*split[0])
    for cut in split[1:]:
        level = level * one(*cut)
    return level


def assign_block(rng, own, number, rows, amount, top, bound, lean):
    ranking = jax.random.permutation(rng, amount)
    packed, ordinary = portions_of(amount, rows * top, bound, lean, True), portions_of(amount, rows * top, bound, lean, False)
    places = jnp.arange(amount)

    def named(tallies, turn):
        used = int((tallies > 0).sum())
        fixed = max(1, used // 4)
        passed = fixed + (places - fixed + turn * (used - fixed)) % max(1, amount - fixed)
        return jnp.zeros((amount,), jnp.int32).at[ranking[jnp.where(places < fixed, places, passed)]].set(jnp.asarray(tallies, jnp.int32))

    tallies = jnp.where(number % 4 == 0, named(packed, number // 4), named(ordinary, number - number // 4 - 1))
    mixed = jax.random.permutation(jax.random.fold_in(own, 3), amount)
    donor, receiver = mixed[0:amount // 2 * 2:2], mixed[1:amount // 2 * 2:2]
    room = jnp.minimum(tallies[donor] - 1, bound - tallies[receiver]) // 2
    room = jnp.where((donor == ranking[0]) | (receiver == ranking[0]) | (tallies[receiver] == 0), 0, jnp.maximum(room, 0))
    passed = jax.random.randint(jax.random.fold_in(own, 4), (amount // 2,), 0, 1 << 20) % (room + 1)
    tallies = tallies.at[donor].add(-passed).at[receiver].add(passed)
    labels = jnp.searchsorted(jnp.cumsum(tallies), jnp.arange(rows * top), side="right").astype(jnp.int32)
    table = labels.reshape(top, rows).T
    table = table[jax.random.permutation(jax.random.fold_in(own, 1), rows)]
    turn = jax.random.randint(jax.random.fold_in(own, 2), (rows, 1), 0, top)
    return jnp.take_along_axis(table, (jnp.arange(top)[None, :] + turn) % top, axis=1)


def portions_of(number_of, total, limit, slope, full):
    loads = [(1 << 20) // math.isqrt(rank ** slope) + 1 for rank in range(1, number_of + 1)]
    largest = limit if full else min(limit, max(-(-total // number_of), total * loads[0] // sum(loads)))
    least = 1 if total - largest >= number_of - 1 else 0
    given, spare = [largest] + [least] * (number_of - 1), total - largest - least * (number_of - 1)
    while spare > 0:
        candidates = [i for i in range(1, number_of) if given[i] < largest] or [i for i in range(1, number_of) if given[i] < limit]
        pool, left = sum([loads[i] for i in candidates]), spare
        for i in candidates:
            extra = min(limit - given[i], max(1, left * loads[i] // pool), spare)
            given[i] = given[i] + extra
            spare = spare - extra
    return np.array(given)


def bell_draw(key, dims, scale, most, split=(), kind=jnp.bfloat16):
    entries = jax.random.normal(key, dims, jnp.float32) * scale
    if len(split) > 0:
        entries = block_levels(key, dims, split, -0.22, 0.18) * entries
    return jnp.clip(entries, min=-most, max=most).astype(kind)


def noise_with(own_key, shape, scale, reach, split, heavy, kind=jnp.bfloat16):
    result = scale * jax.random.normal(own_key, shape, jnp.float32)
    if split:
        result = result * block_levels(own_key, shape, split, -0.22, 0.18)
    return jnp.clip(with_spikes(result, jax.random.fold_in(own_key, 3), *heavy), -reach, reach).astype(kind)


def setup_inputs(seed: int = 0) -> dict:
    seeds = jax.random.split(jax.random.key(seed), 8)
    tokens = noise_with(seeds[0], (TOKENS, D), 1.0, 24.0, ((0, 512),), (0, 1, 512, 6.0))
    cotangent = bell_draw(seeds[1], (TOKENS, D), 1.0, 6.0, ((0, 512),))
    route_keys = jax.random.split(jax.random.fold_in(seeds[2], 1), TOKENS // TOK_DEV)
    route_turns = jax.random.permutation(jax.random.fold_in(seeds[2], 3), TOKENS // TOK_DEV)
    route = jax.vmap(lambda own, number: assign_block(jax.random.fold_in(seeds[2], 2), own, number, TOK_DEV, HOT, 1, CAP, 2))(route_keys, route_turns).reshape((TOKENS, 1))
    prob = jnp.clip(0.049804688 + 0.9501953 * jax.random.uniform(seeds[3], (TOKENS,), jnp.float32) ** block_levels(seeds[3], (TOKENS,), ((0, 512),), -0.2, 0.2), 0.049804688, 1.0).astype(jnp.bfloat16)
    w_gate = bell_draw(seeds[4], (SHARDS, D, FQ), D ** -0.5, 0.125, ((0, 16),), jnp.float32)
    w_up = bell_draw(seeds[5], (SHARDS, D, FQ), D ** -0.5, 0.125, ((0, 16),), jnp.float32)
    w_down = bell_draw(seeds[6], (SHARDS, D, FQ), FF ** -0.5, 0.25, ((0, 16),), jnp.float32)
    return {"tokens": tokens, "cotangent": cotangent, "route": route, "prob": prob, "w_gate": w_gate, "w_up": w_up, "w_down": w_down}


highest = lax.Precision.HIGHEST

def expert_rows(row_tokens, row_cotangents, row_probs, gate_weight, up_weight, down_weight):
    tokens_f32 = row_tokens.astype(jnp.float32)
    cotangent_f32 = row_cotangents.astype(jnp.float32)
    probs_f32 = row_probs.astype(jnp.float32)
    gate_pre = jnp.dot(tokens_f32, gate_weight, precision=highest)
    up_pre = jnp.dot(tokens_f32, up_weight, precision=highest)
    sigmoid_val = jax.nn.sigmoid(gate_pre)
    activation = gate_pre * sigmoid_val
    hidden = activation * up_pre
    backward = jnp.dot(cotangent_f32, down_weight, precision=highest)
    prob_part = lax.optimization_barrier(jnp.sum(hidden * backward, axis=1))
    d_hidden = probs_f32[:, None] * backward
    d_up = d_hidden * activation
    d_gate = d_hidden * up_pre * sigmoid_val * (1.0 + gate_pre * (1.0 - sigmoid_val))
    input_part = jnp.dot(d_gate, gate_weight.T, precision=highest) + jnp.dot(d_up, up_weight.T, precision=highest)
    grad_g = jnp.dot(tokens_f32.T, d_gate, precision=highest)
    grad_u = jnp.dot(tokens_f32.T, d_up, precision=highest)
    grad_d = jnp.dot((probs_f32[:, None] * cotangent_f32).T, hidden, precision=highest)
    return (input_part, prob_part, grad_g, grad_u, grad_d)

def slot_positions(route_column):
    onehot = (route_column[:, None] == jnp.arange(HOT, dtype=jnp.int32)[None, :]).astype(jnp.int32)
    earlier = jnp.cumsum(onehot, axis=0) - onehot
    rank_in_expert = lax.optimization_barrier(jnp.sum(earlier * onehot, axis=1))
    return (route_column * CAP + rank_in_expert).astype(jnp.int32)

def join_quarters(weight):
    quarters = N_EXPERT // HOT
    return weight.reshape(HOT, quarters, D, FF // quarters).transpose(0, 2, 1, 3).reshape(HOT, D, FF)

def split_quarters(weight):
    quarters = N_EXPERT // HOT
    return weight.reshape(HOT, D, quarters, FF // quarters).transpose(0, 2, 1, 3).reshape(HOT * quarters, D, FF // quarters)

def place_rows(values, position):
    empty_rows = jnp.zeros((HOT * CAP,) + values.shape[1:], values.dtype)
    return empty_rows.at[position].set(values)

def take_rows(values, position):
    return values[position]

def reference(tokens, cotangent, route, prob, w_gate, w_up, w_down):
    full_gate = join_quarters(w_gate)
    full_up = join_quarters(w_up)
    full_down = join_quarters(w_down)
    tok_blocks = tokens.reshape(N_DP, N_EXPERT, TOK_DEV, D)
    cot_blocks = cotangent.reshape(N_DP, N_EXPERT, TOK_DEV, D)
    route_blocks = route.reshape(N_DP, N_EXPERT, TOK_DEV).astype(jnp.int32)
    prob_blocks = prob.reshape(N_DP, N_EXPERT, TOK_DEV)

    def block_step(grad_carry, block_data):
        tok_b, cot_b, route_b, prob_b = block_data
        position = jax.vmap(slot_positions)(route_b)
        slot_tok = jax.vmap(place_rows)(tok_b, position)
        slot_cot = jax.vmap(place_rows)(cot_b, position)
        slot_prob = jax.vmap(place_rows)(prob_b, position)
        rows_tok = slot_tok.reshape(N_EXPERT, HOT, CAP, D).transpose(1, 0, 2, 3).reshape(HOT, N_EXPERT * CAP, D)
        rows_cot = slot_cot.reshape(N_EXPERT, HOT, CAP, D).transpose(1, 0, 2, 3).reshape(HOT, N_EXPERT * CAP, D)
        rows_prob = slot_prob.reshape(N_EXPERT, HOT, CAP).transpose(1, 0, 2).reshape(HOT, N_EXPERT * CAP)
        input_part, prob_part, grad_g, grad_u, grad_d = jax.vmap(expert_rows)(rows_tok, rows_cot, rows_prob, full_gate, full_up, full_down)
        input_back = input_part.astype(jnp.bfloat16).reshape(HOT, N_EXPERT, CAP, D).transpose(1, 0, 2, 3).reshape(N_EXPERT, HOT * CAP, D)
        prob_back = prob_part.astype(jnp.bfloat16).reshape(HOT, N_EXPERT, CAP).transpose(1, 0, 2).reshape(N_EXPERT, HOT * CAP)
        grad_in = jax.vmap(take_rows)(input_back, position)
        grad_pr = jax.vmap(take_rows)(prob_back, position)
        new_carry = (grad_carry[0] + grad_g, grad_carry[1] + grad_u, grad_carry[2] + grad_d)
        return (new_carry, (grad_in, grad_pr))
    zero_grads = jnp.zeros((HOT, D, FF), jnp.float32)
    grad_sums, outputs = lax.scan(block_step, (zero_grads, zero_grads, zero_grads), (tok_blocks, cot_blocks, route_blocks, prob_blocks))
    grad_scale = lax.rsqrt(jnp.float32(TOKENS))
    grad_input = outputs[0].reshape(TOKENS, D)
    grad_prob = outputs[1].reshape(TOKENS)
    return (grad_input, grad_prob, split_quarters(grad_sums[0] * grad_scale), split_quarters(grad_sums[1] * grad_scale), split_quarters(grad_sums[2] * grad_scale))
```

```python
import math

import jax
import jax.numpy as jnp
from jax import lax
from jax.experimental import pallas as pl
from jax.experimental.pallas import tpu as pltpu
from jax.sharding import PartitionSpec as P

D = 2048
HOT = 4
CAP = 48
FQ = 128
NX, NYL, NYH, NZ, NC = 4, 4, 2, 8, 2
NY = NYL * NYH
EXTRA = 128
WIDE = D + EXTRA
W_TOP = 32767.0
MESH = pl.DeviceIdType.MESH
f32, bf16, i32 = jnp.float32, jnp.bfloat16, jnp.int32


def coords():
    dp = lax.axis_index("dp")
    ex = lax.axis_index("expert")
    core = lax.rem(dp, NC)
    x = lax.rem(lax.div(dp, NC), NX)
    ylo = lax.div(dp, NC * NX)
    yhi = lax.rem(ex, NYH)
    z = lax.div(ex, NYH)
    return x, yhi * NYL + ylo, z, core


def device(x, y, z, core):
    return ((lax.rem(y, NYL) * NX + x) * NC + core, z * NYH + lax.div(y, NYL))


def slot_route(z, k):
    odd = lax.rem(z, 2)
    sign = 1 - 2 * odd
    to = sign * (k if k % 2 == 0 else -k)
    come = sign * -k
    return lax.rem(z + to + NZ, NZ), lax.rem(z + come + NZ, NZ)


def remote(src, dst, send, recv, dev):
    return pltpu.make_async_remote_copy(
        src_ref=src, dst_ref=dst, send_sem=send, recv_sem=recv, device_id=dev, device_id_type=MESH
    )


def enter(sources, count):
    barrier = pltpu.get_barrier_semaphore()
    for dev in sources:
        pl.semaphore_signal(barrier, inc=1, device_id=dev, device_id_type=MESH)
    pl.semaphore_wait(barrier, count)


def gather_kernel(tok_ref, cot_ref, w_ref, s_ref, rtok_ref, rcot_ref, wall_ref, sall_ref,
                  s_send, s_recv, ds_send, ds_recv, z_send, z_recv, y_send, y_recv, x_send, x_recv, c_send, c_recv, loc):
    x, y, z, c = coords()
    ylo, yhi = lax.rem(y, NYL), lax.div(y, NYL)
    zlo = lax.rem(z, 2)
    zp = z + 1 - 2 * zlo
    right, left = lax.rem(x + 1, NX), lax.rem(x + NX - 1, NX)
    routes = [slot_route(z, k) for k in (1, 2, 3)]
    ys = [lax.rem(y + j, NY) for j in range(1, NY)]
    enter(
        [device(x, y, come, c) for _, come in routes]
        + [device(x, y, zp, c)]
        + [device(x, yy, z, c) for yy in ys]
        + [device(right, y, z, c), device(left, y, z, c), device(x, y, z, 1 - c)],
        3 + 1 + 7 + 2 + 1,
    )
    row = pl.multiple_of(((c * NX + x) * NYL + ylo) * 32, 32)
    quarter = yhi * 2 + zlo
    mine = pl.ds(quarter * 3, 3)
    zc = remote(w_ref, wall_ref.at[mine, pl.ds(row, 32), :], z_send, z_recv, device(x, y, zp, c))
    zc.start()
    sz = remote(s_ref, sall_ref.at[quarter], s_send.at[0], s_recv.at[0], device(x, y, zp, c))
    sz.start()
    own = pltpu.make_async_copy(w_ref, wall_ref.at[mine, pl.ds(row, 32), :], loc.at[0])
    own.start()
    own_s = pltpu.make_async_copy(s_ref, sall_ref.at[quarter], loc.at[3])
    own_s.start()
    tokens = []
    for i, k in enumerate((1, 2, 3)):
        dev = device(x, y, routes[i][0], c)
        for j, (src, dst) in enumerate(((tok_ref, rtok_ref), (cot_ref, rcot_ref))):
            copy = remote(src.at[k], dst.at[k], ds_send.at[i, j], ds_recv.at[i, j], dev)
            copy.start()
            tokens.append(copy)
    own_tok = pltpu.make_async_copy(tok_ref.at[0], rtok_ref.at[0], loc.at[1])
    own_cot = pltpu.make_async_copy(cot_ref.at[0], rcot_ref.at[0], loc.at[2])
    own_tok.start()
    own_cot.start()
    own.wait()
    zc.wait()
    own_s.wait()
    sz.wait()
    block = wall_ref.at[pl.ds(yhi * 6, 6), pl.ds(row, 32), :]
    ycs = []
    for j in range(1, NY):
        copy = remote(block, block, y_send.at[j - 1], y_recv.at[j - 1], device(x, ys[j - 1], z, c))
        copy.start()
        ycs.append(copy)
    pair = sall_ref.at[pl.ds(yhi * 2, 2)]
    sy = remote(pair, pair, s_send.at[1], s_recv.at[1], device(x, ys[3], z, c))
    sy.start()
    for copy in ycs:
        copy.wait()
    sy.wait()

    def part(xx, half):
        start = pl.multiple_of((c * NX + xx) * 128, 128)
        if half is None:
            return wall_ref.at[:, pl.ds(start, 128), :]
        return wall_ref.at[pl.ds(half * 6, 6), pl.ds(start, 128), :]

    to_right = remote(part(x, None), part(x, None), x_send.at[0], x_recv.at[0], device(right, y, z, c))
    to_left = remote(part(x, None), part(x, None), x_send.at[1], x_recv.at[1], device(left, y, z, c))
    to_right.start()
    to_left.start()
    to_right.wait_recv()
    on_right = remote(part(left, 0), part(left, 0), x_send.at[2], x_recv.at[2], device(right, y, z, c))
    on_right.start()
    to_left.wait_recv()
    on_left = remote(part(right, 1), part(right, 1), x_send.at[3], x_recv.at[3], device(left, y, z, c))
    on_left.start()
    on_right.wait_recv()
    on_left.wait_recv()
    half = wall_ref.at[:, pl.ds(pl.multiple_of(c * 512, 512), 512), :]
    cc = remote(half, half, c_send, c_recv, device(x, y, z, 1 - c))
    cc.start()
    for copy in (to_right, to_left, on_right, on_left):
        copy.wait_send()
    cc.wait()
    for copy in tokens:
        copy.wait()
    own_tok.wait()
    own_cot.wait()


def gather(slot_tok, slot_cot, w_chunk, scales):
    vmem = pl.BlockSpec(memory_space=pltpu.VMEM)
    anyspace = pl.BlockSpec(memory_space=pl.ANY)
    dma = pltpu.SemaphoreType.DMA
    return pl.pallas_call(
        gather_kernel,
        out_shape=[
            jax.ShapeDtypeStruct(slot_tok.shape, slot_tok.dtype),
            jax.ShapeDtypeStruct(slot_cot.shape, slot_cot.dtype),
            jax.ShapeDtypeStruct((12, D // 2, FQ), w_chunk.dtype),
            jax.ShapeDtypeStruct((4, 8, FQ), f32),
        ],
        in_specs=[vmem] * 4,
        out_specs=[anyspace] * 4,
        scratch_shapes=[dma((2,)), dma((2,)), dma((3, 2)), dma((3, 2)), dma, dma, dma((7,)), dma((7,)), dma((4,)), dma((4,)), dma, dma,
                        dma((4,))],
        compiler_params=pltpu.CompilerParams(collective_id=0, has_side_effects=True),
    )(slot_tok, slot_cot, w_chunk, scales)


def scatter_kernel(dx_ref, g_ref, back_ref, out_ref,
                   c_in, x_out, x_in, x_mid, y_out, y_in, z_out, z_in, gbuf,
                   r_send, r_recv, c_send, c_recv, x_send, x_recv, y_send, y_recv, z_send, z_recv, loc):
    x, y, z, c = coords()
    ylo, yhi = lax.rem(y, NYL), lax.div(y, NYL)
    zlo = lax.rem(z, 2)
    zp = z + 1 - 2 * zlo
    right, left = lax.rem(x + 1, NX), lax.rem(x + NX - 1, NX)
    far = lax.rem(x + 2, NX)
    routes = [slot_route(z, k) for k in (1, 2, 3)]
    ys = [lax.rem(y + j, NY) for j in range(1, NY)]
    enter(
        [device(x, y, to, c) for to, _ in routes]
        + [device(x, y, zp, c)]
        + [device(x, yy, z, c) for yy in ys]
        + [device(right, y, z, c), device(left, y, z, c), device(x, y, z, 1 - c)],
        3 + 1 + 7 + 2 + 1,
    )
    cc = remote(g_ref.at[:, 1 - c], c_in, c_send, c_recv, device(x, y, z, 1 - c))
    cc.start()
    mine = pltpu.make_async_copy(g_ref.at[:, c], gbuf, loc.at[0])
    mine.start()
    returns = []
    for i, k in enumerate((1, 2, 3)):
        copy = remote(dx_ref.at[k], back_ref.at[k], r_send.at[i], r_recv.at[i], device(x, y, routes[i][1], c))
        copy.start()
        returns.append(copy)
    own = pltpu.make_async_copy(dx_ref.at[0], back_ref.at[0], loc.at[1])
    own.start()
    mine.wait()
    cc.wait()
    acc = lambda g, xx: gbuf[g * NX + xx] + c_in[g * NX + xx]

    def fill_far(g, _):
        x_out[0, g] = acc(g, far).astype(bf16)
        return 0

    lax.fori_loop(0, 48, fill_far, 0)
    far_right = remote(x_out.at[0, pl.ds(0, 24)], x_mid.at[pl.ds(0, 24)], x_send.at[0], x_recv.at[0],
                       device(right, y, z, c))
    far_left = remote(x_out.at[0, pl.ds(24, 24)], x_mid.at[pl.ds(24, 24)], x_send.at[1], x_recv.at[1],
                      device(left, y, z, c))
    far_right.start()
    far_left.start()

    def fill_plain(g, _):
        x_out[2, g] = acc(24 + g, right).astype(bf16)
        x_out[3, g] = acc(g, left).astype(bf16)
        return 0

    lax.fori_loop(0, 24, fill_plain, 0)
    plain_right = remote(x_out.at[2, pl.ds(0, 24)], x_in.at[0, pl.ds(24, 24)], x_send.at[2], x_recv.at[2],
                         device(right, y, z, c))
    plain_left = remote(x_out.at[3, pl.ds(0, 24)], x_in.at[1, pl.ds(0, 24)], x_send.at[3], x_recv.at[3],
                        device(left, y, z, c))
    plain_right.start()
    plain_left.start()
    far_right.wait_recv()
    far_left.wait_recv()

    def fill_near(g, _):
        x_out[1, g] = (acc(g, right) + x_mid[g].astype(f32)).astype(bf16)
        x_out[1, 24 + g] = (acc(24 + g, left) + x_mid[24 + g].astype(f32)).astype(bf16)
        return 0

    lax.fori_loop(0, 24, fill_near, 0)
    sum_right = remote(x_out.at[1, pl.ds(0, 24)], x_in.at[0, pl.ds(0, 24)], x_send.at[4], x_recv.at[4],
                       device(right, y, z, c))
    sum_left = remote(x_out.at[1, pl.ds(24, 24)], x_in.at[1, pl.ds(24, 24)], x_send.at[5], x_recv.at[5],
                      device(left, y, z, c))
    sum_right.start()
    sum_left.start()
    for copy in (plain_right, plain_left, sum_right, sum_left):
        copy.wait_recv()

    def fill_y(g, _):
        total = acc(g, x) + x_in[0, g].astype(f32) + x_in[1, g].astype(f32)
        gbuf[g * NX + x] = total
        y_out[lax.div(g, 24), lax.rem(lax.div(g, 4), 6), lax.rem(g, 4)] = total.astype(bf16)
        return 0

    lax.fori_loop(0, 48, fill_y, 0)
    ycs = []
    for j in range(1, NY):
        yy = ys[j - 1]
        copy = remote(y_out.at[lax.div(yy, NYL), :, lax.rem(yy, NYL)], y_in.at[j - 1], y_send.at[j - 1],
                      y_recv.at[j - 1], device(x, yy, z, c))
        copy.start()
        ycs.append(copy)
    for copy in ycs:
        copy.wait_recv()

    def fill_z(g, _):
        total = gbuf[((yhi * 6 + g) * NYL + ylo) * NX + x]
        for j in range(NY - 1):
            total = total + y_in[j, g].astype(f32)
        z_out[lax.div(g, 3), lax.rem(g, 3)] = total
        return 0

    lax.fori_loop(0, 6, fill_z, 0)
    zc = remote(z_out.at[1 - zlo], z_in, z_send, z_recv, device(x, y, zp, c))
    zc.start()
    zc.wait_recv()
    scale = 1.0 / math.sqrt(NX * NY * NZ * NC * 128)
    for m in range(3):
        out_ref[m] = (z_out[zlo, m] + z_in[m]) * scale
    for copy in returns:
        copy.wait()
    own.wait()
    zc.wait_send()
    for copy in ycs + [far_right, far_left, plain_right, plain_left, sum_right, sum_left]:
        copy.wait_send()


def scatter(dx, grads):
    vmem = pl.BlockSpec(memory_space=pltpu.VMEM)
    anyspace = pl.BlockSpec(memory_space=pl.ANY)
    dma = pltpu.SemaphoreType.DMA
    return pl.pallas_call(
        scatter_kernel,
        out_shape=[
            jax.ShapeDtypeStruct(dx.shape, dx.dtype),
            jax.ShapeDtypeStruct((3, 64, FQ), f32),
        ],
        in_specs=[vmem, anyspace],
        out_specs=[anyspace, vmem],
        scratch_shapes=[
            pltpu.VMEM((192, 64, FQ), f32),
            pltpu.VMEM((4, 48, 64, FQ), bf16),
            pltpu.VMEM((2, 48, 64, FQ), bf16),
            pltpu.VMEM((48, 64, FQ), bf16),
            pltpu.VMEM((2, 6, 4, 64, FQ), bf16),
            pltpu.VMEM((7, 6, 64, FQ), bf16),
            pltpu.VMEM((2, 3, 64, FQ), f32),
            pltpu.VMEM((3, 64, FQ), f32),
            pltpu.VMEM((192, 64, FQ), f32),
            dma((3,)), dma((3,)), dma, dma, dma((6,)), dma((6,)), dma((7,)), dma((7,)), dma, dma, dma((2,)),
        ],
        compiler_params=pltpu.CompilerParams(
            collective_id=1, has_side_effects=True, vmem_limit_bytes=48 * 1024 * 1024
        ),
    )(dx, grads)


def split(v):
    hi = lax.reduce_precision(v, 8, 7)
    return hi.astype(bf16), (v - hi).astype(bf16)


def dot(a, b, dims):
    return lax.dot_general(a, b, (dims, ((), ())), preferred_element_type=f32)


def shards(tokens, cotangent, route, prob, w_gate, w_up, w_down):
    x, y, z, c = coords()
    odd = lax.rem(z, 2)
    turn = lax.rem(route[:, 0] - lax.div(z, 2) + HOT, HOT)
    slot = jnp.where(turn == 0, 0, jnp.where(turn == 1, 2 - odd, jnp.where(turn == 2, 3, 1 + odd)))
    onehot = (slot[:, None] == jnp.arange(HOT, dtype=jnp.int32)[None, :]).astype(f32)
    before = (jnp.arange(128)[:, None] > jnp.arange(128)[None, :]).astype(bf16)
    earlier = jnp.dot(before, onehot.astype(bf16), preferred_element_type=f32)
    rank = jnp.sum(earlier * onehot, axis=1).astype(jnp.int32)
    position = slot * CAP + rank
    placing = (jnp.arange(HOT * CAP, dtype=jnp.int32)[:, None] == position[None, :]).astype(bf16)
    taking = (position[:, None] == jnp.arange(HOT * CAP, dtype=jnp.int32)[None, :]).astype(bf16)
    wide = jnp.concatenate([tokens, jnp.broadcast_to(prob[:, None], (128, EXTRA))], axis=1)
    slot_tok = jnp.dot(placing, wide, preferred_element_type=f32).astype(bf16).reshape(HOT, CAP, WIDE)
    slot_cot = jnp.dot(placing, cotangent, preferred_element_type=f32).astype(bf16).reshape(HOT, CAP, D)
    row = ((c * NX + x) * NYL + lax.rem(y, NYL)) * 32
    tops = [jnp.maximum(jnp.max(jnp.abs(w[0]), axis=0), 1e-30) for w in (w_gate, w_up, w_down)]
    steps = jnp.stack([t * (1.0 / W_TOP) for t in tops])
    chunk = jnp.stack([lax.dynamic_slice(w[0].reshape(2, D // 2, FQ), (0, row, 0), (2, 32, FQ))
                       for w in (w_gate, w_up, w_down)])
    units = jnp.clip(jnp.round(chunk / steps[:, None, None, :]), -W_TOP, W_TOP).astype(i32)
    packed = units[:, 0] * 65536 + (units[:, 1] + 32768)
    rtok, rcot, wall, sall = gather(slot_tok, slot_cot, packed, jnp.pad(steps, ((0, 5), (0, 0))))

    rows = HOT * CAP
    rtok = rtok.reshape(rows, WIDE)
    toks, probs = rtok[:, :D], rtok[:, D:D + 1].astype(f32)
    cots = rcot.reshape(rows, D)
    wall = wall.reshape(4, 3, D // 2, FQ).transpose(1, 2, 0, 3).reshape(3, D // 2, 4 * FQ)
    full = jnp.concatenate([wall >> 16, (wall & 65535) - 32768], axis=1).astype(f32)
    hi, lo = split(full)
    step = sall[:, :3].transpose(1, 0, 2).reshape(3, 1, 4 * FQ)
    ahead = ((1,), (0,))
    gate_pre = (dot(toks, hi[0], ahead) + dot(toks, lo[0], ahead)) * step[0]
    up_pre = (dot(toks, hi[1], ahead) + dot(toks, lo[1], ahead)) * step[1]
    backward = (dot(cots, hi[2], ahead) + dot(cots, lo[2], ahead)) * step[2]
    sig = jax.nn.sigmoid(gate_pre)
    act = gate_pre * sig
    hidden = act * up_pre
    grad_prob = jnp.sum(hidden * backward, axis=1, keepdims=True)
    d_hidden = probs * backward
    d_up = d_hidden * act
    d_gate = d_hidden * up_pre * sig * (1.0 + gate_pre * (1.0 - sig))
    gh, gl = split(d_gate)
    uh, ul = split(d_up)
    hh, hl = split(probs * hidden)
    turned = ((1,), (1,))
    sgh, sgl = split(d_gate * step[0])
    suh, sul = split(d_up * step[1])
    dx = (
        dot(sgh, hi[0], turned) + dot(sgh, lo[0], turned) + dot(sgl, hi[0], turned)
        + dot(suh, hi[1], turned) + dot(suh, lo[1], turned) + dot(sul, hi[1], turned)
    )
    dx = jnp.concatenate([dx, jnp.broadcast_to(grad_prob, (rows, EXTRA))], axis=1).astype(bf16)

    def weight_grad(left, h, l):
        both = dot(left, h, ((0,), (0,))) + dot(left, l, ((0,), (0,)))
        return both.reshape(D, 4, FQ).transpose(1, 0, 2)

    grads = jnp.stack([weight_grad(toks, gh, gl), weight_grad(toks, uh, ul), weight_grad(cots, hh, hl)], axis=1)
    back, mine = scatter(dx.reshape(HOT, CAP, WIDE), grads.reshape(192, 2, 64, FQ))
    out = jnp.dot(taking, back.reshape(rows, WIDE), preferred_element_type=f32).astype(bf16)
    return (out[:, :D], out[:, D], mine[0][None], mine[1][None], mine[2][None])


def solution(mesh):
    rows = P(("dp", "expert"), None)
    placed = (rows, rows, rows, P(("dp", "expert")), P("expert", None, None), P("expert", None, None),
              P("expert", None, None))
    return jax.shard_map(
        shards,
        mesh=mesh,
        in_specs=placed,
        out_specs=(rows, P(("dp", "expert")), P("expert", "dp", None), P("expert", "dp", None),
                   P("expert", "dp", None)),
        check_vma=False,
    )
```

```python
import math

import jax
import jax.numpy as jnp
from jax import lax
from jax.experimental import pallas as pl
from jax.experimental.pallas import tpu as pltpu
from jax.sharding import PartitionSpec as P

D = 2048
HOT = 4
CAP = 48
FQ = 128
NX, NYL, NYH, NZ, NC = 4, 4, 2, 8, 2
NY = NYL * NYH
EXTRA = 128
ROWS = HOT * CAP
PAIR = 2 * FQ
WIDE = D + EXTRA
W_TOP = 32767.0
MESH = pl.DeviceIdType.MESH
f32, bf16, i32 = jnp.float32, jnp.bfloat16, jnp.int32


def coords():
    dp = lax.axis_index("dp")
    ex = lax.axis_index("expert")
    core = lax.rem(dp, NC)
    x = lax.rem(lax.div(dp, NC), NX)
    ylo = lax.div(dp, NC * NX)
    yhi = lax.rem(ex, NYH)
    z = lax.div(ex, NYH)
    return x, yhi * NYL + ylo, z, core


def device(x, y, z, core):
    return ((lax.rem(y, NYL) * NX + x) * NC + core, z * NYH + lax.div(y, NYL))


def slot_route(z, k):
    odd = lax.rem(z, 2)
    sign = 1 - 2 * odd
    to = sign * (k if k % 2 == 0 else -k)
    come = sign * -k
    return lax.rem(z + to + NZ, NZ), lax.rem(z + come + NZ, NZ)


def remote(src, dst, send, recv, dev):
    return pltpu.make_async_remote_copy(
        src_ref=src, dst_ref=dst, send_sem=send, recv_sem=recv, device_id=dev, device_id_type=MESH
    )


def enter(sources, count):
    barrier = pltpu.get_barrier_semaphore()
    for dev in sources:
        pl.semaphore_signal(barrier, inc=1, device_id=dev, device_id_type=MESH)
    pl.semaphore_wait(barrier, count)


def dot(a, b, dims):
    return lax.dot_general(a, b, (dims, ((), ())), preferred_element_type=f32)


def halves(v):
    hi = v.astype(bf16)
    return hi, (v - hi.astype(f32)).astype(bf16)


def layer_kernel(tok_ref, cot_ref, w_ref, s_ref, back_ref, out_ref,
                 rtok, rcot, wall, sall, whi, wlo, dhi, dlo, shi, slo, dxb, gprob,
                 g, c_in, x_out, x_in, x_mid, total, y_out, y_in, z_out, z_in,
                 s_send, s_recv, t_send, t_recv, wz_send, wz_recv, wy_send, wy_recv, wx_send, wx_recv, wc_send, wc_recv,
                 r_send, r_recv, c_send, c_recv, x_send, x_recv, y_send, y_recv, z_send, z_recv, loc):
    x, y, z, c = coords()
    ylo, yhi = lax.rem(y, NYL), lax.div(y, NYL)
    zlo = lax.rem(z, 2)
    zp = z + 1 - 2 * zlo
    right, left = lax.rem(x + 1, NX), lax.rem(x + NX - 1, NX)
    far = lax.rem(x + 2, NX)
    routes = [slot_route(z, k) for k in (1, 2, 3)]
    ys = [lax.rem(y + j, NY) for j in range(1, NY)]
    to_dev = [device(x, y, to, c) for to, _ in routes]
    come_dev = [device(x, y, come, c) for _, come in routes]
    pair_dev = device(x, y, zp, c)
    y_dev = [device(x, yy, z, c) for yy in ys]
    right_dev, left_dev, core_dev = device(right, y, z, c), device(left, y, z, c), device(x, y, z, 1 - c)
    enter([to_dev[0], to_dev[1], come_dev[1], to_dev[2], pair_dev] + y_dev + [right_dev, left_dev, core_dev], 15)

    row = pl.multiple_of(((c * NX + x) * NYL + ylo) * 32, 32)
    quarter = yhi * 2 + zlo
    mine = wall.at[pl.ds(quarter * 3, 3), pl.ds(row, 32), :]
    wz = remote(w_ref, mine, wz_send, wz_recv, pair_dev)
    wz.start()
    sz = remote(s_ref, sall.at[quarter], s_send.at[0], s_recv.at[0], pair_dev)
    sz.start()
    locals_ = [
        pltpu.make_async_copy(w_ref, mine, loc.at[0]),
        pltpu.make_async_copy(s_ref, sall.at[quarter], loc.at[1]),
        pltpu.make_async_copy(tok_ref.at[pl.ds(0, CAP)], rtok.at[pl.ds(0, CAP)], loc.at[2]),
        pltpu.make_async_copy(cot_ref.at[pl.ds(0, CAP)], rcot.at[pl.ds(0, CAP)], loc.at[3]),
    ]
    for copy in locals_:
        copy.start()
    tokens = []
    for i, k in enumerate((1, 2, 3)):
        for j, (src, dst) in enumerate(((tok_ref, rtok), (cot_ref, rcot))):
            at = pl.ds(k * CAP, CAP)
            copy = remote(src.at[at], dst.at[at], t_send.at[i, j], t_recv.at[i, j], to_dev[i])
            copy.start()
            tokens.append(copy)
    for copy in locals_:
        copy.wait()
    wz.wait()
    sz.wait()
    block = wall.at[pl.ds(yhi * 6, 6), pl.ds(row, 32), :]
    wys = [remote(block, block, wy_send.at[j], wy_recv.at[j], y_dev[j]) for j in range(7)]
    for copy in wys:
        copy.start()
    both = sall.at[pl.ds(yhi * 2, 2)]
    sy = remote(both, both, s_send.at[1], s_recv.at[1], y_dev[3])
    sy.start()
    for copy in wys:
        copy.wait()
    sy.wait()

    def part(xx, lo, n):
        return wall.at[pl.ds(lo, n), pl.ds(pl.multiple_of((c * NX + xx) * 128, 128), 128), :]

    to_right = remote(part(x, 0, 12), part(x, 0, 12), wx_send.at[0], wx_recv.at[0], right_dev)
    to_left = remote(part(x, 0, 12), part(x, 0, 12), wx_send.at[1], wx_recv.at[1], left_dev)
    to_right.start()
    to_left.start()
    to_right.wait_recv()
    on_right = remote(part(left, 0, 6), part(left, 0, 6), wx_send.at[2], wx_recv.at[2], right_dev)
    on_right.start()
    to_left.wait_recv()
    on_left = remote(part(right, 6, 6), part(right, 6, 6), wx_send.at[3], wx_recv.at[3], left_dev)
    on_left.start()
    on_right.wait_recv()
    on_left.wait_recv()
    half = wall.at[:, pl.ds(pl.multiple_of(c * 512, 512), 512), :]
    wc = remote(half, half, wc_send, wc_recv, core_dev)
    wc.start()

    def unpack(base):
        def step(t, _):
            mp, at = lax.div(t, 4), pl.multiple_of(base + lax.rem(t, 4) * 128, 128)
            p, m = lax.div(mp, 3), lax.rem(mp, 3)
            for q in range(2):
                v = wall[(p * 2 + q) * 3 + m, pl.ds(at, 128), :]
                for start, u in ((0, v >> 16), (D // 2, (v & 65535) - 32768)):
                    hi, lo = halves(u.astype(f32))
                    whi[mp, pl.ds(pl.multiple_of(start + at, 128), 128), q * FQ:(q + 1) * FQ] = hi
                    wlo[mp, pl.ds(pl.multiple_of(start + at, 128), 128), q * FQ:(q + 1) * FQ] = lo
            return 0

        lax.fori_loop(0, 24, step, 0)

    unpack(c * 512)
    wc.wait_recv()
    unpack((1 - c) * 512)
    for copy in tokens:
        copy.wait_recv()

    gprob[...] = jnp.zeros_like(gprob)

    def forward(p, _):
        def pre(left, m):
            step = jnp.concatenate([sall[p * 2, pl.ds(m, 1), :], sall[p * 2 + 1, pl.ds(m, 1), :]], axis=1)
            both = dot(left, whi[p * 3 + m], ((1,), (0,))) + dot(left, wlo[p * 3 + m], ((1,), (0,)))
            return both * step, step

        toks = rtok[:, :D]
        gate_pre, gate_step = pre(toks, 0)
        up_pre, up_step = pre(toks, 1)
        backward, _ = pre(rcot[...], 2)
        pr = rtok[:, D:].astype(f32)
        pr = jnp.concatenate([pr, pr], axis=1)
        sig = jax.nn.sigmoid(gate_pre)
        act = gate_pre * sig
        hidden = act * up_pre
        gprob[...] += jnp.broadcast_to(jnp.sum(hidden * backward, axis=1, keepdims=True), (ROWS, EXTRA))
        d_hidden = pr * backward
        d_up = d_hidden * act
        d_gate = d_hidden * up_pre * sig * (1.0 + gate_pre * (1.0 - sig))
        for m, v in enumerate((d_gate, d_up, pr * hidden)):
            hi, lo = halves(v)
            dhi[p * 3 + m] = hi
            dlo[p * 3 + m] = lo
        for m, v in enumerate((d_gate * gate_step, d_up * up_step)):
            hi, lo = halves(v)
            shi[p * 2 + m] = hi
            slo[p * 2 + m] = lo
        return 0

    lax.fori_loop(0, 2, forward, 0)

    def weight_grad(m, left):
        def step(n, _):
            lt = left[:, pl.ds(pl.multiple_of(n * 256, 256), 256)]
            for p in range(2):
                v = dot(lt, dhi[p * 3 + m], ((0,), (0,))) + dot(lt, dlo[p * 3 + m], ((0,), (0,)))
                for q in range(2):
                    for i in range(4):
                        g[m, (p * 2 + q) * 16 + n * 2 + i // 2, i % 2] = v[i * 64:(i + 1) * 64, q * FQ:(q + 1) * FQ]
            return 0

        lax.fori_loop(0, 8, step, 0)

    def core_start(m):
        copy = remote(g.at[m, :, 1 - c], c_in.at[m], c_send.at[m], c_recv.at[m], core_dev)
        copy.start()
        return copy

    def acc(m, gq, xx):
        return g[m, gq * NX + xx, c] + c_in[m, gq * NX + xx]

    def x_first(m):
        def fill_far(i, _):
            x_out[m, 0, i] = acc(m, i, far).astype(bf16)
            return 0

        lax.fori_loop(0, 16, fill_far, 0)
        fr = remote(x_out.at[m, 0, pl.ds(0, 8)], x_mid.at[m, pl.ds(0, 8)], x_send.at[m, 0], x_recv.at[m, 0], right_dev)
        fl = remote(x_out.at[m, 0, pl.ds(8, 8)], x_mid.at[m, pl.ds(8, 8)], x_send.at[m, 1], x_recv.at[m, 1], left_dev)
        fr.start()
        fl.start()

        def fill_plain(i, _):
            x_out[m, 2, i] = acc(m, 8 + i, right).astype(bf16)
            x_out[m, 3, i] = acc(m, i, left).astype(bf16)
            return 0

        lax.fori_loop(0, 8, fill_plain, 0)
        pr = remote(x_out.at[m, 2, pl.ds(0, 8)], x_in.at[m, 0, pl.ds(8, 8)], x_send.at[m, 2], x_recv.at[m, 2], right_dev)
        pl_ = remote(x_out.at[m, 3, pl.ds(0, 8)], x_in.at[m, 1, pl.ds(0, 8)], x_send.at[m, 3], x_recv.at[m, 3], left_dev)
        pr.start()
        pl_.start()
        return [fr, fl, pr, pl_]

    def x_second(m, first):
        first[0].wait_recv()
        first[1].wait_recv()

        def fill_near(i, _):
            x_out[m, 1, i] = (acc(m, i, right) + x_mid[m, i].astype(f32)).astype(bf16)
            x_out[m, 1, 8 + i] = (acc(m, 8 + i, left) + x_mid[m, 8 + i].astype(f32)).astype(bf16)
            return 0

        lax.fori_loop(0, 8, fill_near, 0)
        sr = remote(x_out.at[m, 1, pl.ds(0, 8)], x_in.at[m, 0, pl.ds(0, 8)], x_send.at[m, 4], x_recv.at[m, 4], right_dev)
        sl = remote(x_out.at[m, 1, pl.ds(8, 8)], x_in.at[m, 1, pl.ds(8, 8)], x_send.at[m, 5], x_recv.at[m, 5], left_dev)
        sr.start()
        sl.start()
        return first + [sr, sl]

    def y_start(m, xs):
        for copy in xs[2:]:
            copy.wait_recv()

        def fill(i, _):
            v = acc(m, i, x) + x_in[m, 0, i].astype(f32) + x_in[m, 1, i].astype(f32)
            total[m, i] = v
            y_out[m, lax.div(i, 8), lax.rem(lax.div(i, 4), 2), lax.rem(i, 4)] = v.astype(bf16)
            return 0

        lax.fori_loop(0, 16, fill, 0)
        copies = []
        for j in range(7):
            src = y_out.at[m, lax.div(ys[j], NYL), :, lax.rem(ys[j], NYL)]
            copies.append(remote(src, y_in.at[m, j], y_send.at[m, j], y_recv.at[m, j], y_dev[j]))
            copies[-1].start()
        return copies

    def z_start(m, ycs):
        for copy in ycs:
            copy.wait_recv()

        def fill(i, _):
            v = total[m, (yhi * 2 + i) * NYL + ylo]
            for j in range(7):
                v = v + y_in[m, j, i].astype(f32)
            z_out[m, i] = v
            return 0

        lax.fori_loop(0, 2, fill, 0)
        copy = remote(z_out.at[m, 1 - zlo], z_in.at[m], z_send.at[m], z_recv.at[m], pair_dev)
        copy.start()
        return copy

    weight_grad(2, rcot)
    c2 = core_start(2)
    weight_grad(0, rtok)
    c0 = core_start(0)
    c2.wait_recv()
    x2 = x_first(2)
    weight_grad(1, rtok)
    c1 = core_start(1)
    c0.wait_recv()
    x0 = x_first(0)

    def input_grad(n, _):
        at = pl.ds(pl.multiple_of(n * 256, 256), 256)
        v = jnp.zeros((ROWS, 256), f32)
        for p in range(2):
            for m in range(2):
                hi, lo = whi[p * 3 + m, at, :], wlo[p * 3 + m, at, :]
                v += dot(shi[p * 2 + m], hi, ((1,), (1,)))
                v += dot(shi[p * 2 + m], lo, ((1,), (1,)))
                v += dot(slo[p * 2 + m], hi, ((1,), (1,)))
        dxb[:, at] = v.astype(bf16)
        return 0

    lax.fori_loop(0, 8, input_grad, 0)
    dxb[:, D:] = gprob[...].astype(bf16)
    returns = []
    for i, k in enumerate((1, 2, 3)):
        at = pl.ds(k * CAP, CAP)
        returns.append(remote(dxb.at[at], back_ref.at[at], r_send.at[i], r_recv.at[i], come_dev[i]))
        returns[-1].start()
    own = pltpu.make_async_copy(dxb.at[pl.ds(0, CAP)], back_ref.at[pl.ds(0, CAP)], loc.at[4])
    own.start()
    x2 = x_second(2, x2)
    c1.wait_recv()
    x1 = x_first(1)
    x0 = x_second(0, x0)
    y2 = y_start(2, x2)
    x1 = x_second(1, x1)
    y0 = y_start(0, x0)
    z2 = z_start(2, y2)
    y1 = y_start(1, x1)
    z0 = z_start(0, y0)
    z1 = z_start(1, y1)
    scale = 1.0 / math.sqrt(NX * NY * NZ * NC * 128)
    for m, copy in ((2, z2), (0, z0), (1, z1)):
        copy.wait_recv()
        out_ref[m] = (z_out[m, zlo] + z_in[m]) * scale
    for copy in returns:
        copy.wait()
    own.wait()
    for copy in tokens + [to_right, to_left, on_right, on_left, wc, c0, c1, c2] + x0 + x1 + x2 + y0 + y1 + y2 + [z0, z1, z2]:
        copy.wait_send()


def layer(slot_tok, slot_cot, packed, steps):
    vmem = pl.BlockSpec(memory_space=pltpu.VMEM)
    dma = pltpu.SemaphoreType.DMA
    V = pltpu.VMEM
    return pl.pallas_call(
        layer_kernel,
        out_shape=[
            jax.ShapeDtypeStruct((ROWS, WIDE), bf16),
            jax.ShapeDtypeStruct((3, 64, FQ), f32),
        ],
        in_specs=[vmem] * 4,
        out_specs=[vmem] * 2,
        scratch_shapes=[
            V((ROWS, WIDE), bf16), V((ROWS, D), bf16), V((12, D // 2, FQ), i32), V((4, 8, FQ), f32),
            V((6, D, PAIR), bf16), V((6, D, PAIR), bf16),
            V((6, ROWS, PAIR), bf16), V((6, ROWS, PAIR), bf16), V((4, ROWS, PAIR), bf16), V((4, ROWS, PAIR), bf16),
            V((ROWS, WIDE), bf16), V((ROWS, EXTRA), f32),
            V((3, 64, 2, 64, FQ), f32), V((3, 64, 64, FQ), f32),
            V((3, 4, 16, 64, FQ), bf16), V((3, 2, 16, 64, FQ), bf16), V((3, 16, 64, FQ), bf16),
            V((3, 16, 64, FQ), f32), V((3, 2, 2, 4, 64, FQ), bf16), V((3, 7, 2, 64, FQ), bf16),
            V((3, 2, 64, FQ), f32), V((3, 64, FQ), f32),
            dma((2,)), dma((2,)), dma((3, 2)), dma((3, 2)), dma, dma, dma((7,)), dma((7,)), dma((4,)), dma((4,)), dma, dma,
            dma((3,)), dma((3,)), dma((3,)), dma((3,)), dma((3, 6)), dma((3, 6)), dma((3, 7)), dma((3, 7)),
            dma((3,)), dma((3,)), dma((5,)),
        ],
        compiler_params=pltpu.CompilerParams(
            collective_id=0, has_side_effects=True, vmem_limit_bytes=62 * 1024 * 1024
        ),
    )(slot_tok, slot_cot, packed, steps)


def shards(tokens, cotangent, route, prob, w_gate, w_up, w_down):
    x, y, z, c = coords()
    odd = lax.rem(z, 2)
    turn = lax.rem(route[:, 0] - lax.div(z, 2) + HOT, HOT)
    slot = jnp.where(turn == 0, 0, jnp.where(turn == 1, 2 - odd, jnp.where(turn == 2, 3, 1 + odd)))
    onehot = (slot[:, None] == jnp.arange(HOT, dtype=jnp.int32)[None, :]).astype(f32)
    before = (jnp.arange(128)[:, None] > jnp.arange(128)[None, :]).astype(bf16)
    earlier = jnp.dot(before, onehot.astype(bf16), preferred_element_type=f32)
    rank = jnp.sum(earlier * onehot, axis=1).astype(jnp.int32)
    position = slot * CAP + rank
    placing = (jnp.arange(HOT * CAP, dtype=jnp.int32)[:, None] == position[None, :]).astype(bf16)
    taking = (position[:, None] == jnp.arange(HOT * CAP, dtype=jnp.int32)[None, :]).astype(bf16)
    wide = jnp.concatenate([tokens, jnp.broadcast_to(prob[:, None], (128, EXTRA))], axis=1)
    slot_tok = jnp.dot(placing, wide, preferred_element_type=f32).astype(bf16)
    slot_cot = jnp.dot(placing, cotangent, preferred_element_type=f32).astype(bf16)
    row = ((c * NX + x) * NYL + lax.rem(y, NYL)) * 32
    tops = [jnp.maximum(jnp.max(jnp.abs(w[0]), axis=0), 1e-30) for w in (w_gate, w_up, w_down)]
    steps = jnp.stack([t * (1.0 / W_TOP) for t in tops])
    chunk = jnp.stack([lax.dynamic_slice(w[0].reshape(2, D // 2, FQ), (0, row, 0), (2, 32, FQ))
                       for w in (w_gate, w_up, w_down)])
    units = jnp.clip(jnp.round(chunk / steps[:, None, None, :]), -W_TOP, W_TOP).astype(i32)
    packed = units[:, 0] * 65536 + (units[:, 1] + 32768)
    back, mine = layer(slot_tok, slot_cot, packed, jnp.pad(steps, ((0, 5), (0, 0))))
    out = jnp.dot(taking, back, preferred_element_type=f32).astype(bf16)
    return (out[:, :D], out[:, D], mine[0][None], mine[1][None], mine[2][None])


def solution(mesh):
    rows = P(("dp", "expert"), None)
    placed = (rows, rows, rows, P(("dp", "expert")), P("expert", None, None), P("expert", None, None),
              P("expert", None, None))
    return jax.shard_map(
        shards,
        mesh=mesh,
        in_specs=placed,
        out_specs=(rows, P(("dp", "expert")), P("expert", "dp", None), P("expert", "dp", None),
                   P("expert", "dp", None)),
        check_vma=False,
    )
```

```python
import math

import jax
import jax.numpy as jnp
from jax import lax
from jax.experimental import pallas as pl
from jax.experimental.pallas import tpu as pltpu
from jax.sharding import PartitionSpec as P

D = 2048
HOT = 4
CAP = 48
FQ = 128
NX, NYL, NYH, NZ, NC = 4, 4, 2, 8, 2
NY = NYL * NYH
EXTRA = 128
ROWS = HOT * CAP
PAIR = 2 * FQ
WIDE = D + EXTRA
W_TOP = 32767.0
MESH = pl.DeviceIdType.MESH
f32, bf16, i32 = jnp.float32, jnp.bfloat16, jnp.int32


def coords():
    dp = lax.axis_index("dp")
    ex = lax.axis_index("expert")
    core = lax.rem(dp, NC)
    x = lax.rem(lax.div(dp, NC), NX)
    ylo = lax.div(dp, NC * NX)
    yhi = lax.rem(ex, NYH)
    z = lax.div(ex, NYH)
    return x, yhi * NYL + ylo, z, core


def device(x, y, z, core):
    return ((lax.rem(y, NYL) * NX + x) * NC + core, z * NYH + lax.div(y, NYL))


def slot_route(z, k):
    odd = lax.rem(z, 2)
    sign = 1 - 2 * odd
    to = sign * (k if k % 2 == 0 else -k)
    come = sign * -k
    return lax.rem(z + to + NZ, NZ), lax.rem(z + come + NZ, NZ)


def remote(src, dst, send, recv, dev):
    return pltpu.make_async_remote_copy(
        src_ref=src, dst_ref=dst, send_sem=send, recv_sem=recv, device_id=dev, device_id_type=MESH
    )


def enter(sources, count):
    barrier = pltpu.get_barrier_semaphore()
    for dev in sources:
        pl.semaphore_signal(barrier, inc=1, device_id=dev, device_id_type=MESH)
    pl.semaphore_wait(barrier, count)


def dot(a, b, dims):
    return lax.dot_general(a, b, (dims, ((), ())), preferred_element_type=f32)


def halves(v):
    hi = v.astype(bf16)
    return hi, (v - hi.astype(f32)).astype(bf16)


def layer_kernel(tok_ref, cot_ref, w_ref, s_ref, back_ref, out_ref,
                 rtok, rcot, wall, sall, whi, wlo, dhi, dlo, shi, slo, dxb, gprob,
                 g, c_in, x_out, x_in, x_mid, y_own, y_out, y_in, z_out, z_in,
                 s_send, s_recv, t_send, t_recv, wz_send, wz_recv, wy_send, wy_recv, wx_send, wx_recv, wc_send, wc_recv,
                 r_send, r_recv, c_send, c_recv, x_send, x_recv, y_send, y_recv, z_send, z_recv, loc):
    x, y, z, c = coords()
    ylo, yhi = lax.rem(y, NYL), lax.div(y, NYL)
    zlo = lax.rem(z, 2)
    zp = z + 1 - 2 * zlo
    right, left = lax.rem(x + 1, NX), lax.rem(x + NX - 1, NX)
    far = lax.rem(x + 2, NX)
    routes = [slot_route(z, k) for k in (1, 2, 3)]
    ys = [lax.rem(y + j, NY) for j in range(1, NY)]
    to_dev = [device(x, y, to, c) for to, _ in routes]
    come_dev = [device(x, y, come, c) for _, come in routes]
    pair_dev = device(x, y, zp, c)
    y_dev = [device(x, yy, z, c) for yy in ys]
    right_dev, left_dev, core_dev = device(right, y, z, c), device(left, y, z, c), device(x, y, z, 1 - c)
    enter([to_dev[0], to_dev[1], come_dev[1], to_dev[2], pair_dev] + y_dev + [right_dev, left_dev, core_dev], 15)

    quarter = yhi * 2 + zlo
    up_dev, down_dev = y_dev[0], y_dev[6]

    def rows_at(start, n):
        return pl.ds(pl.multiple_of(start, 16), n)

    def y0_block(yy, lo, n):
        return wall.at[pl.ds(lax.div(yy, NYL) * 6 + lo, n), rows_at(((c * NX + x) * NYL + lax.rem(yy, NYL)) * 16, 16), :]

    def x0_block(xx, lo, n):
        return wall.at[pl.ds(lo, n), rows_at((c * NX + xx) * 64, 64), :]

    def x1_block(xx, lo, n):
        return wall.at[pl.ds(yhi * 6 + lo, n), rows_at(512 + ((c * NYL + ylo) * NX + xx) * 16, 16), :]

    def y1_block(yy, lo, n):
        return wall.at[pl.ds(lax.div(yy, NYL) * 6 + lo, n), rows_at(512 + (c * NYL + lax.rem(yy, NYL)) * 64, 64), :]

    mine = [
        wall.at[pl.ds(quarter * 3, 3), rows_at(((c * NX + x) * NYL + ylo) * 16, 16), :],
        wall.at[pl.ds(quarter * 3, 3), rows_at(512 + ((c * NYL + ylo) * NX + x) * 16, 16), :],
    ]
    wz = [remote(w_ref.at[h], mine[h], wz_send.at[h], wz_recv.at[h], pair_dev) for h in range(2)]
    sz = remote(s_ref, sall.at[quarter], s_send.at[0], s_recv.at[0], pair_dev)
    for copy in wz + [sz]:
        copy.start()
    locals_ = [
        pltpu.make_async_copy(w_ref.at[0], mine[0], loc.at[0]),
        pltpu.make_async_copy(w_ref.at[1], mine[1], loc.at[5]),
        pltpu.make_async_copy(s_ref, sall.at[quarter], loc.at[1]),
        pltpu.make_async_copy(tok_ref.at[pl.ds(0, CAP)], rtok.at[pl.ds(0, CAP)], loc.at[2]),
        pltpu.make_async_copy(cot_ref.at[pl.ds(0, CAP)], rcot.at[pl.ds(0, CAP)], loc.at[3]),
    ]
    for copy in locals_:
        copy.start()
    tokens = []
    for i, k in enumerate((1, 2, 3)):
        for j, (src, dst) in enumerate(((tok_ref, rtok), (cot_ref, rcot))):
            at = pl.ds(k * CAP, CAP)
            copy = remote(src.at[at], dst.at[at], t_send.at[i, j], t_recv.at[i, j], to_dev[i])
            copy.start()
            tokens.append(copy)
    for copy in locals_:
        copy.wait()
    sent = []

    def start(src, send, recv, dev):
        copy = remote(src, src, send, recv, dev)
        copy.start()
        sent.append(copy)
        return copy

    def y_hop(block, h, d, whole):
        back, ahead = lax.rem(y - d + NY, NY), lax.rem(y + d, NY)
        first, second = (block(back, 0, 6), block(ahead, 0, 6)) if whole else (block(back, 0, 3), block(ahead, 3, 3))
        return [
            start(first, wy_send.at[h, 2 * d], wy_recv.at[h, 2 * d], up_dev),
            start(second, wy_send.at[h, 2 * d + 1], wy_recv.at[h, 2 * d + 1], down_dev),
        ]

    def x_hop(block, h, n):
        return [
            start(block(x, 0, n), wx_send.at[h, 0], wx_recv.at[h, 0], right_dev),
            start(block(x, 0, n), wx_send.at[h, 1], wx_recv.at[h, 1], left_dev),
        ]

    def x_relay(block, h, n):
        return [
            start(block(left, 0, n // 2), wx_send.at[h, 2], wx_recv.at[h, 2], right_dev),
            start(block(right, n // 2, n // 2), wx_send.at[h, 3], wx_recv.at[h, 3], left_dev),
        ]

    def arrived(copies):
        for copy in copies:
            copy.wait_recv()

    def core_send(h):
        return start(wall.at[:, rows_at(h * 512 + c * 256, 256), :], wc_send.at[h], wc_recv.at[h], core_dev)

    wz[0].wait()
    ya = y_hop(y0_block, 0, 0, True)
    wz[1].wait()
    xa = x_hop(x1_block, 1, 6)
    sz.wait()
    sy = start(sall.at[pl.ds(yhi * 2, 2)], s_send.at[1], s_recv.at[1], y_dev[3])
    arrived(ya)
    ya = y_hop(y0_block, 0, 1, True)
    arrived(xa)
    xa = x_relay(x1_block, 1, 6)
    arrived(ya)
    ya = y_hop(y0_block, 0, 2, True)
    arrived(xa)
    yb = y_hop(y1_block, 1, 0, True)
    arrived(ya)
    ya = y_hop(y0_block, 0, 3, False)
    arrived(ya)
    xb = x_hop(x0_block, 0, 12)
    arrived(yb)
    yb = y_hop(y1_block, 1, 1, True)
    arrived(xb)
    xb = x_relay(x0_block, 0, 12)
    arrived(yb)
    yb = y_hop(y1_block, 1, 2, True)
    arrived(xb)
    wc0 = core_send(0)

    def unpack(base):
        def step(t, _):
            mp, at = lax.div(t, 2), pl.multiple_of(base + lax.rem(t, 2) * 128, 128)
            p, m = lax.div(mp, 3), lax.rem(mp, 3)
            for q in range(2):
                v = wall[(q * 2 + p) * 3 + m, pl.ds(at, 128), :]
                for begin, u in ((0, v >> 16), (D // 2, (v & 65535) - 32768)):
                    hi, lo = halves(u.astype(f32))
                    whi[mp, pl.ds(pl.multiple_of(begin + at, 128), 128), q * FQ:(q + 1) * FQ] = hi
                    wlo[mp, pl.ds(pl.multiple_of(begin + at, 128), 128), q * FQ:(q + 1) * FQ] = lo
            return 0

        lax.fori_loop(0, 12, step, 0)

    arrived(yb)
    yb = y_hop(y1_block, 1, 3, False)
    unpack(c * 256)
    arrived(yb)
    wc1 = core_send(1)
    unpack(512 + c * 256)
    wc0.wait_recv()
    unpack((1 - c) * 256)
    wc1.wait_recv()
    unpack(512 + (1 - c) * 256)
    sy.wait_recv()
    arrived(tokens)

    gprob[...] = jnp.zeros_like(gprob)

    def forward(p):
        def pre(left, m):
            step = jnp.concatenate([sall[p, pl.ds(m, 1), :], sall[2 + p, pl.ds(m, 1), :]], axis=1)
            both = dot(left, whi[p * 3 + m], ((1,), (0,))) + dot(left, wlo[p * 3 + m], ((1,), (0,)))
            return both * step, step

        toks = rtok[:, :D]
        gate_pre, gate_step = pre(toks, 0)
        up_pre, up_step = pre(toks, 1)
        backward, _ = pre(rcot[...], 2)
        pr = rtok[:, D:].astype(f32)
        pr = jnp.concatenate([pr, pr], axis=1)
        sig = jax.nn.sigmoid(gate_pre)
        act = gate_pre * sig
        hidden = act * up_pre
        gprob[...] += jnp.broadcast_to(jnp.sum(hidden * backward, axis=1, keepdims=True), (ROWS, EXTRA))
        d_hidden = pr * backward
        d_up = d_hidden * act
        d_gate = d_hidden * up_pre * sig * (1.0 + gate_pre * (1.0 - sig))
        for m, v in enumerate((d_gate, d_up, pr * hidden)):
            hi, lo = halves(v)
            dhi[p * 3 + m] = hi
            dlo[p * 3 + m] = lo
        for m, v in enumerate((d_gate * gate_step, d_up * up_step)):
            hi, lo = halves(v)
            shi[p * 2 + m] = hi
            slo[p * 2 + m] = lo

    def weight_grad(p, m, left_ref):
        def step(n, _):
            lt = left_ref[:, pl.ds(pl.multiple_of(n * 256, 256), 256)]
            v = dot(lt, dhi[p * 3 + m], ((0,), (0,))) + dot(lt, dlo[p * 3 + m], ((0,), (0,)))
            for q in range(2):
                for i in range(4):
                    g[p * 3 + m, q * 16 + n * 2 + i // 2, i % 2] = v[i * 64:(i + 1) * 64, q * FQ:(q + 1) * FQ]
            return 0

        lax.fori_loop(0, 8, step, 0)
        copy = remote(g.at[p * 3 + m, :, 1 - c], c_in.at[p * 3 + m], c_send.at[p * 3 + m], c_recv.at[p * 3 + m], core_dev)
        copy.start()
        sent.append(copy)
        return copy

    def acc(k, yy, xx):
        return g[k, yy * NX + xx, c] + c_in[k, yy * NX + xx]

    def push(k, src, dst, n, dev):
        copy = remote(src, dst, x_send.at[k, n], x_recv.at[k, n], dev)
        copy.start()
        sent.append(copy)
        return copy

    first, second = pl.ds(0, 4), pl.ds(4, 4)

    def x_first(k, came):
        came.wait_recv()

        def fill_far(i, _):
            x_out[k, 0, i] = acc(k, i, far).astype(bf16)
            return 0

        lax.fori_loop(0, 8, fill_far, 0)
        fr = push(k, x_out.at[k, 0, first], x_mid.at[k, first], 0, right_dev)
        fl = push(k, x_out.at[k, 0, second], x_mid.at[k, second], 1, left_dev)

        def fill_plain(i, _):
            x_out[k, 2, i] = acc(k, 4 + i, right).astype(bf16)
            x_out[k, 3, i] = acc(k, i, left).astype(bf16)
            return 0

        lax.fori_loop(0, 4, fill_plain, 0)
        nr = push(k, x_out.at[k, 2, first], x_in.at[k, 0, second], 2, right_dev)
        nl = push(k, x_out.at[k, 3, first], x_in.at[k, 1, first], 3, left_dev)
        return [fr, fl], [nr, nl]

    def x_second(k, xs):
        arrived(xs[0])

        def fill_near(i, _):
            x_out[k, 1, i] = (acc(k, i, right) + x_mid[k, i].astype(f32)).astype(bf16)
            x_out[k, 1, 4 + i] = (acc(k, 4 + i, left) + x_mid[k, 4 + i].astype(f32)).astype(bf16)
            return 0

        lax.fori_loop(0, 4, fill_near, 0)
        return xs[1] + [
            push(k, x_out.at[k, 1, first], x_in.at[k, 0, first], 4, right_dev),
            push(k, x_out.at[k, 1, second], x_in.at[k, 1, second], 5, left_dev),
        ]

    def y_start(k, xs):
        arrived(xs)

        def total(i):
            return acc(k, i, x) + x_in[k, 0, i].astype(f32) + x_in[k, 1, i].astype(f32)

        def fill(i, _):
            y_out[k, i] = total(i).astype(bf16)
            return 0

        lax.fori_loop(0, 8, fill, 0)
        copies = [remote(y_out.at[k, ys[j]], y_in.at[k, j], y_send.at[k, j], y_recv.at[k, j], y_dev[j]) for j in range(7)]
        for copy in copies:
            copy.start()
        sent.extend(copies)
        y_own[k] = total(y)
        return copies

    def z_start(m, ycs):
        for p in range(2):
            arrived(ycs[p])
            v = y_own[p * 3 + m]
            for j in range(7):
                v = v + y_in[p * 3 + m, j].astype(f32)
            z_out[m, p] = v
        copy = remote(z_out.at[m, 1 - zlo], z_in.at[m], z_send.at[m], z_recv.at[m], pair_dev)
        copy.start()
        sent.append(copy)
        return copy

    def input_grad(n, _):
        at = pl.ds(pl.multiple_of(n * 256, 256), 256)
        v = jnp.zeros((ROWS, 256), f32)
        for p in range(2):
            for m in range(2):
                hi, lo = whi[p * 3 + m, at, :], wlo[p * 3 + m, at, :]
                v += dot(shi[p * 2 + m], hi, ((1,), (1,)))
                v += dot(shi[p * 2 + m], lo, ((1,), (1,)))
                v += dot(slo[p * 2 + m], hi, ((1,), (1,)))
        dxb[:, at] = v.astype(bf16)
        return 0

    forward(0)
    c02 = weight_grad(0, 2, rcot)
    c00 = weight_grad(0, 0, rtok)
    x02 = x_first(2, c02)
    c01 = weight_grad(0, 1, rtok)
    x00 = x_first(0, c00)
    forward(1)
    x02 = x_second(2, x02)
    x01 = x_first(1, c01)
    c12 = weight_grad(1, 2, rcot)
    x00 = x_second(0, x00)
    c10 = weight_grad(1, 0, rtok)
    y02 = y_start(2, x02)
    x01 = x_second(1, x01)
    x12 = x_first(5, c12)
    c11 = weight_grad(1, 1, rtok)
    y00 = y_start(0, x00)
    x10 = x_first(3, c10)
    lax.fori_loop(0, 4, input_grad, 0)
    x12 = x_second(5, x12)
    x11 = x_first(4, c11)
    y01 = y_start(1, x01)
    lax.fori_loop(4, 8, input_grad, 0)
    dxb[:, D:] = gprob[...].astype(bf16)
    returns = []
    for i, k in enumerate((1, 2, 3)):
        at = pl.ds(k * CAP, CAP)
        returns.append(remote(dxb.at[at], back_ref.at[at], r_send.at[i], r_recv.at[i], come_dev[i]))
        returns[-1].start()
    own = pltpu.make_async_copy(dxb.at[pl.ds(0, CAP)], back_ref.at[pl.ds(0, CAP)], loc.at[4])
    own.start()
    x10 = x_second(3, x10)
    y12 = y_start(5, x12)
    x11 = x_second(4, x11)
    y10 = y_start(3, x10)
    z2 = z_start(2, (y02, y12))
    y11 = y_start(4, x11)
    z0 = z_start(0, (y00, y10))
    z1 = z_start(1, (y01, y11))
    scale = 1.0 / math.sqrt(NX * NY * NZ * NC * 128)
    for m, copy in ((2, z2), (0, z0), (1, z1)):
        copy.wait_recv()
        out_ref[m] = (z_out[m, zlo] + z_in[m]) * scale
    for copy in returns:
        copy.wait()
    own.wait()
    for copy in tokens + sent:
        copy.wait_send()


def layer(slot_tok, slot_cot, packed, steps):
    vmem = pl.BlockSpec(memory_space=pltpu.VMEM)
    dma = pltpu.SemaphoreType.DMA
    V = pltpu.VMEM
    return pl.pallas_call(
        layer_kernel,
        out_shape=[
            jax.ShapeDtypeStruct((ROWS, WIDE), bf16),
            jax.ShapeDtypeStruct((3, 64, FQ), f32),
        ],
        in_specs=[vmem] * 4,
        out_specs=[vmem] * 2,
        scratch_shapes=[
            V((ROWS, WIDE), bf16), V((ROWS, D), bf16), V((12, D // 2, FQ), i32), V((4, 8, FQ), f32),
            V((6, D, PAIR), bf16), V((6, D, PAIR), bf16),
            V((6, ROWS, PAIR), bf16), V((6, ROWS, PAIR), bf16), V((4, ROWS, PAIR), bf16), V((4, ROWS, PAIR), bf16),
            V((ROWS, WIDE), bf16), V((ROWS, EXTRA), f32),
            V((6, 32, 2, 64, FQ), f32), V((6, 32, 64, FQ), f32),
            V((6, 4, 8, 64, FQ), bf16), V((6, 2, 8, 64, FQ), bf16), V((6, 8, 64, FQ), bf16),
            V((6, 64, FQ), f32), V((6, 8, 64, FQ), bf16), V((6, 7, 64, FQ), bf16),
            V((3, 2, 64, FQ), f32), V((3, 64, FQ), f32),
            dma((2,)), dma((2,)), dma((3, 2)), dma((3, 2)), dma((2,)), dma((2,)), dma((2, 8)), dma((2, 8)), dma((2, 4)),
            dma((2, 4)), dma((2,)), dma((2,)), dma((3,)), dma((3,)), dma((6,)), dma((6,)), dma((6, 6)), dma((6, 6)),
            dma((6, 7)), dma((6, 7)), dma((3,)), dma((3,)), dma((6,)),
        ],
        compiler_params=pltpu.CompilerParams(
            collective_id=0, has_side_effects=True, vmem_limit_bytes=62 * 1024 * 1024
        ),
    )(slot_tok, slot_cot, packed, steps)


def shards(tokens, cotangent, route, prob, w_gate, w_up, w_down):
    x, y, z, c = coords()
    odd = lax.rem(z, 2)
    turn = lax.rem(route[:, 0] - lax.div(z, 2) + HOT, HOT)
    slot = jnp.where(turn == 0, 0, jnp.where(turn == 1, 2 - odd, jnp.where(turn == 2, 3, 1 + odd)))
    onehot = (slot[:, None] == jnp.arange(HOT, dtype=jnp.int32)[None, :]).astype(f32)
    before = (jnp.arange(128)[:, None] > jnp.arange(128)[None, :]).astype(bf16)
    earlier = jnp.dot(before, onehot.astype(bf16), preferred_element_type=f32)
    rank = jnp.sum(earlier * onehot, axis=1).astype(jnp.int32)
    position = slot * CAP + rank
    placing = (jnp.arange(HOT * CAP, dtype=jnp.int32)[:, None] == position[None, :]).astype(bf16)
    taking = (position[:, None] == jnp.arange(HOT * CAP, dtype=jnp.int32)[None, :]).astype(bf16)
    wide = jnp.concatenate([tokens, jnp.broadcast_to(prob[:, None], (128, EXTRA))], axis=1)
    slot_tok = jnp.dot(placing, wide, preferred_element_type=f32).astype(bf16)
    slot_cot = jnp.dot(placing, cotangent, preferred_element_type=f32).astype(bf16)
    ylo = lax.rem(y, NYL)
    starts = (((c * NX + x) * NYL + ylo) * 16, 512 + ((c * NYL + ylo) * NX + x) * 16)
    weights = (w_gate, w_up, w_down)
    tops = [jnp.maximum(jnp.max(jnp.abs(w[0]), axis=0), 1e-30) for w in weights]
    steps = jnp.stack([t * (1.0 / W_TOP) for t in tops])
    chunk = jnp.stack([
        jnp.stack([lax.dynamic_slice(w[0].reshape(2, D // 2, FQ), (0, start, 0), (2, 16, FQ)) for w in weights])
        for start in starts
    ])
    units = jnp.clip(jnp.round(chunk / steps[None, :, None, None, :]), -W_TOP, W_TOP).astype(i32)
    packed = units[:, :, 0] * 65536 + (units[:, :, 1] + 32768)
    back, mine = layer(slot_tok, slot_cot, packed, jnp.pad(steps, ((0, 5), (0, 0))))
    out = jnp.dot(taking, back, preferred_element_type=f32).astype(bf16)
    return (out[:, :D], out[:, D], mine[0][None], mine[1][None], mine[2][None])


def solution(mesh):
    rows = P(("dp", "expert"), None)
    placed = (rows, rows, rows, P(("dp", "expert")), P("expert", None, None), P("expert", None, None),
              P("expert", None, None))
    return jax.shard_map(
        shards,
        mesh=mesh,
        in_specs=placed,
        out_specs=(rows, P(("dp", "expert")), P("expert", "dp", None), P("expert", "dp", None),
                   P("expert", "dp", None)),
        check_vma=False,
    )
```

```python
import math

import jax
import jax.numpy as jnp
from jax import lax
from jax.experimental import pallas as pl
from jax.experimental.pallas import tpu as pltpu
from jax.sharding import PartitionSpec as P

D = 2048
HOT = 4
CAP = 48
FQ = 128
NX, NYL, NYH, NZ, NC = 4, 4, 2, 8, 2
NY = NYL * NYH
EXTRA = 128
ROWS = HOT * CAP
PAIR = 2 * FQ
WIDE = D + EXTRA
W_TOP = 32767.0
MESH = pl.DeviceIdType.MESH
f32, bf16, i32 = jnp.float32, jnp.bfloat16, jnp.int32


def coords():
    dp = lax.axis_index("dp")
    ex = lax.axis_index("expert")
    core = lax.rem(dp, NC)
    x = lax.rem(lax.div(dp, NC), NX)
    ylo = lax.div(dp, NC * NX)
    yhi = lax.rem(ex, NYH)
    z = lax.div(ex, NYH)
    return x, yhi * NYL + ylo, z, core


def device(x, y, z, core):
    return ((lax.rem(y, NYL) * NX + x) * NC + core, z * NYH + lax.div(y, NYL))


def slot_route(z, k):
    odd = lax.rem(z, 2)
    sign = 1 - 2 * odd
    to = sign * (k if k % 2 == 0 else -k)
    come = sign * -k
    return lax.rem(z + to + NZ, NZ), lax.rem(z + come + NZ, NZ)


def remote(src, dst, send, recv, dev):
    return pltpu.make_async_remote_copy(
        src_ref=src, dst_ref=dst, send_sem=send, recv_sem=recv, device_id=dev, device_id_type=MESH
    )


def enter(sources, count, meanwhile):
    barrier = pltpu.get_barrier_semaphore()
    for dev in sources:
        pl.semaphore_signal(barrier, inc=1, device_id=dev, device_id_type=MESH)
    meanwhile()
    pl.semaphore_wait(barrier, count)


def dot(a, b, dims):
    return lax.dot_general(a, b, (dims, ((), ())), preferred_element_type=f32)


def halves(v):
    hi = v.astype(bf16)
    return hi, (v - hi.astype(f32)).astype(bf16)


def layer_kernel(info_ref, tokens_ref, cots_ref, w_ref, s_ref, back_ref, backp_ref, out_ref,
                 tok_ref, cot_ref, tok_t, cot_t, rtok, rcot, wall, sall, whi, wlo, dhi, dlo, shi, slo, dxb, dpb, gprob,
                 g, c_in, x_out, x_in, x_mid, y_own, y_out, y_in, z_out, z_in,
                 s_send, s_recv, t_send, t_recv, wz_send, wz_recv, wd_send, wd_recv, wy_send, wy_recv, wx_send, wx_recv, wc_send, wc_recv,
                 r_send, r_recv, c_send, c_recv, x_send, x_recv, y_send, y_recv, z_send, z_recv, loc):
    x, y, z, c = coords()
    ylo, yhi = lax.rem(y, NYL), lax.div(y, NYL)
    zlo = lax.rem(z, 2)
    zp = z + 1 - 2 * zlo
    right, left = lax.rem(x + 1, NX), lax.rem(x + NX - 1, NX)
    far = lax.rem(x + 2, NX)
    routes = [slot_route(z, k) for k in (1, 2, 3)]
    ys = [lax.rem(y + j, NY) for j in range(1, NY)]
    to_dev = [device(x, y, to, c) for to, _ in routes]
    come_dev = [device(x, y, come, c) for _, come in routes]
    pair_dev = device(x, y, zp, c)
    y_dev = [device(x, yy, z, c) for yy in ys]
    right_dev, left_dev, core_dev = device(right, y, z, c), device(left, y, z, c), device(x, y, z, 1 - c)
    def place():
        here = lax.broadcasted_iota(jnp.int32, (ROWS, 128), 0).astype(f32) == info_ref[0:1, :]
        prob = jnp.sum(jnp.where(here, info_ref[1:2, :], 0.0), axis=1, keepdims=True)
        placing = here.astype(f32).astype(bf16)
        tok_ref[:, :D] = dot(placing, tokens_ref[...], ((1,), (0,))).astype(bf16)
        tok_ref[:, D:] = jnp.broadcast_to(prob, (ROWS, EXTRA)).astype(bf16)
        cot_ref[...] = dot(placing, cots_ref[...], ((1,), (0,))).astype(bf16)

    enter([to_dev[0], to_dev[1], come_dev[1], to_dev[2], pair_dev] + y_dev + [right_dev, left_dev, core_dev], 15, place)

    up_dev, down_dev = y_dev[0], y_dev[6]

    def rows_at(start, n):
        return pl.ds(pl.multiple_of(start, 16), n)

    def y0_block(s, yy):
        return wall.at[pl.ds(s * 6 + lax.div(yy, NYL) * 3, 3), rows_at(((c * NX + x) * NYL + lax.rem(yy, NYL)) * 16, 16), :]

    def x0_block(s, xx, lo, n):
        return wall.at[pl.ds(s * 6 + lo, n), rows_at((c * NX + xx) * 64, 64), :]

    def x1_block(s, xx, lo, n):
        return wall.at[pl.ds(s * 6 + yhi * 3 + lo, n), rows_at(512 + ((c * NYL + ylo) * NX + xx) * 16, 16), :]

    def y1_block(s, yy, lo, n):
        return wall.at[pl.ds(s * 6 + lax.div(yy, NYL) * 3, 3), rows_at(512 + (c * NYL + lax.rem(yy, NYL)) * 64 + lo, n), :]

    mine = pl.ds((zlo * 2 + yhi) * 3, 3)
    places = [
        wall.at[mine, rows_at(((c * NX + x) * NYL + ylo) * 16, 16), :],
        wall.at[mine, rows_at(512 + ((c * NYL + ylo) * NX + x) * 16, 16), :],
    ]
    wz = [remote(w_ref.at[h], places[h], wz_send.at[h], wz_recv.at[h], pair_dev) for h in range(2)]
    sz = remote(s_ref, sall.at[zlo, yhi], s_send.at[0], s_recv.at[0], pair_dev)
    for copy in wz + [sz]:
        copy.start()
    tokens = []
    for j, (src, dst) in enumerate(((tok_ref, rtok), (cot_ref, rcot))):
        for i, k in enumerate((3, 1, 2)):
            at = pl.ds(k * CAP, CAP)
            copy = remote(src.at[at], dst.at[at], t_send.at[i, j], t_recv.at[i, j], to_dev[k - 1])
            copy.start()
            tokens.append(copy)
    locals_ = [
        pltpu.make_async_copy(w_ref.at[0], places[0], loc.at[0]),
        pltpu.make_async_copy(w_ref.at[1], places[1], loc.at[1]),
        pltpu.make_async_copy(s_ref, sall.at[zlo, yhi], loc.at[2]),
    ]
    for copy in locals_:
        copy.start()
    sent = []

    def start(src, send, recv, dev):
        copy = remote(src, src, send, recv, dev)
        copy.start()
        sent.append(copy)
        return copy

    def y_direct(i, s):
        return [start(y0_block(s, y), wd_send.at[i, j], wd_recv.at[i, j], y_dev[j]) for j in range(7)]

    def y_hop(i, s, d):
        back, ahead = lax.rem(y - d + NY, NY), lax.rem(y + d, NY)
        one, two = (y1_block(s, back, 0, 64), y1_block(s, ahead, 0, 64)) if d < 3 else (
            y1_block(s, back, 0, 32), y1_block(s, ahead, 32, 32))
        return [
            start(one, wy_send.at[i, 2 * d], wy_recv.at[i, 2 * d], up_dev),
            start(two, wy_send.at[i, 2 * d + 1], wy_recv.at[i, 2 * d + 1], down_dev),
        ]

    def x_hop(block, i, s, n):
        return [
            start(block(s, x, 0, n), wx_send.at[i, 0], wx_recv.at[i, 0], right_dev),
            start(block(s, x, 0, n), wx_send.at[i, 1], wx_recv.at[i, 1], left_dev),
        ]

    def x_relay(block, i, s, n):
        cut = n // 2
        return [
            start(block(s, left, 0, cut), wx_send.at[i, 2], wx_recv.at[i, 2], right_dev),
            start(block(s, right, cut, n - cut), wx_send.at[i, 3], wx_recv.at[i, 3], left_dev),
        ]

    def arrived(copies):
        for copy in copies:
            copy.wait_recv()

    def core_send(i, h, s):
        return start(wall.at[pl.ds(s * 6, 6), rows_at(h * 512 + c * 256, 256), :], wc_send.at[i], wc_recv.at[i], core_dev)

    sa, sb = zlo, 1 - zlo
    for copy in locals_:
        copy.wait()
    ya = y_direct(0, sa)
    xa = x_hop(x1_block, 2, sa, 3)
    wz[0].wait()
    yb = y_direct(1, sb)
    wz[1].wait()
    xb = x_hop(x1_block, 3, sb, 3)
    sz.wait()
    mates = sall.at[:, yhi]
    sy = start(mates, s_send.at[1], s_recv.at[1], y_dev[3])
    rtok[pl.ds(0, CAP), :] = tok_ref[pl.ds(0, CAP), :]
    rcot[pl.ds(0, CAP), :] = cot_ref[pl.ds(0, CAP), :]

    arrived(xa)
    xa = x_relay(x1_block, 2, sa, 3)
    arrived(xb)
    xb = x_relay(x1_block, 3, sb, 3)
    arrived(ya)
    x0a = x_hop(x0_block, 0, sa, 6)
    arrived(xa)
    y1a = y_hop(0, sa, 0)
    arrived(xb)
    y1b = y_hop(1, sb, 0)
    arrived(yb)
    x0b = x_hop(x0_block, 1, sb, 6)
    arrived(y1a)
    y1a = y_hop(0, sa, 1)
    arrived(y1b)
    y1b = y_hop(1, sb, 1)
    arrived(x0a)
    x0a = x_relay(x0_block, 0, sa, 6)
    arrived(y1a)
    y1a = y_hop(0, sa, 2)
    arrived(y1b)
    y1b = y_hop(1, sb, 2)
    arrived(x0b)
    x0b = x_relay(x0_block, 1, sb, 6)
    arrived(x0a)
    wcs = [core_send(0, 0, sa)]
    arrived(y1a)
    y1a = y_hop(0, sa, 3)
    arrived(y1b)
    y1b = y_hop(1, sb, 3)
    arrived(x0b)
    wcs.append(core_send(1, 0, sb))
    arrived(y1a)
    wcs.append(core_send(2, 1, sa))
    arrived(y1b)
    wcs.append(core_send(3, 1, sb))

    def unpack(base):
        def step(t, _):
            mp, at = lax.div(t, 2), pl.multiple_of(base + lax.rem(t, 2) * 128, 128)
            p, m = lax.div(mp, 3), lax.rem(mp, 3)
            for q in range(2):
                v = wall[(p * 2 + q) * 3 + m, pl.ds(at, 128), :]
                for begin, u in ((0, v >> 16), (D // 2, (v & 65535) - 32768)):
                    hi, lo = halves(u.astype(f32))
                    whi[mp, pl.ds(pl.multiple_of(begin + at, 128), 128), q * FQ:(q + 1) * FQ] = hi
                    wlo[mp, pl.ds(pl.multiple_of(begin + at, 128), 128), q * FQ:(q + 1) * FQ] = lo
            return 0

        lax.fori_loop(0, 12, step, 0)

    unpack(c * 256)
    unpack(512 + c * 256)
    arrived(tokens[:3])

    def turn(left_ref, out_t):
        def step(n, _):
            at = pl.ds(pl.multiple_of(n * 256, 256), 256)
            out_t[at, :] = jnp.transpose(left_ref[:, at])
            return 0

        lax.fori_loop(0, 8, step, 0)

    turn(rtok, tok_t)
    arrived(wcs)
    unpack((1 - c) * 256)
    unpack(512 + (1 - c) * 256)
    sy.wait_recv()

    gprob[...] = jnp.zeros_like(gprob)

    def forward(p):
        def pre(left, m):
            step = jnp.concatenate([sall[p, 0, pl.ds(m, 1), :], sall[p, 1, pl.ds(m, 1), :]], axis=1)
            both = dot(left, whi[p * 3 + m], ((1,), (0,))) + dot(left, wlo[p * 3 + m], ((1,), (0,)))
            return both * step, step

        toks = rtok[:, :D]
        gate_pre, gate_step = pre(toks, 0)
        up_pre, up_step = pre(toks, 1)
        if p == 0:
            arrived(tokens[3:])
        backward, _ = pre(rcot[...], 2)
        pr = rtok[:, D:].astype(f32)
        pr = jnp.concatenate([pr, pr], axis=1)
        sig = jax.nn.sigmoid(gate_pre)
        act = gate_pre * sig
        hidden = act * up_pre
        gprob[...] += jnp.broadcast_to(jnp.sum(hidden * backward, axis=1, keepdims=True), (ROWS, EXTRA))
        d_hidden = pr * backward
        d_up = d_hidden * act
        d_gate = d_hidden * up_pre * sig * (1.0 + gate_pre * (1.0 - sig))
        for m, v in enumerate((d_gate, d_up, pr * hidden)):
            hi, lo = halves(v)
            dhi[p * 3 + m] = hi
            dlo[p * 3 + m] = lo
        for m, v in enumerate((d_gate * gate_step, d_up * up_step)):
            hi, lo = halves(v)
            shi[p * 2 + m] = hi
            slo[p * 2 + m] = lo

    def weight_grad(p, m, left_ref):
        def step(n, _):
            lt = left_ref[pl.ds(pl.multiple_of(n * 256, 256), 256), :]
            v = dot(lt, dhi[p * 3 + m], ((1,), (0,))) + dot(lt, dlo[p * 3 + m], ((1,), (0,)))
            for q in range(2):
                for i in range(4):
                    g[p * 3 + m, q * 16 + n * 2 + i // 2, i % 2] = v[i * 64:(i + 1) * 64, q * FQ:(q + 1) * FQ]
            return 0

        lax.fori_loop(0, 8, step, 0)
        copy = remote(g.at[p * 3 + m, :, 1 - c], c_in.at[p * 3 + m], c_send.at[p * 3 + m], c_recv.at[p * 3 + m], core_dev)
        copy.start()
        sent.append(copy)
        return copy

    def acc(k, yy, xx):
        return g[k, yy * NX + xx, c] + c_in[k, yy * NX + xx]

    def push(k, src, dst, n, dev):
        copy = remote(src, dst, x_send.at[k, n], x_recv.at[k, n], dev)
        copy.start()
        sent.append(copy)
        return copy

    first, second = pl.ds(0, 4), pl.ds(4, 4)

    def x_first(k, came):
        came.wait_recv()

        def fill_far(i, _):
            x_out[k, 0, i] = acc(k, i, far).astype(bf16)
            return 0

        lax.fori_loop(0, 8, fill_far, 0)
        fr = push(k, x_out.at[k, 0, first], x_mid.at[k, first], 0, right_dev)
        fl = push(k, x_out.at[k, 0, second], x_mid.at[k, second], 1, left_dev)

        def fill_plain(i, _):
            x_out[k, 2, i] = acc(k, 4 + i, right).astype(bf16)
            x_out[k, 3, i] = acc(k, i, left).astype(bf16)
            return 0

        lax.fori_loop(0, 4, fill_plain, 0)
        nr = push(k, x_out.at[k, 2, first], x_in.at[k, 0, second], 2, right_dev)
        nl = push(k, x_out.at[k, 3, first], x_in.at[k, 1, first], 3, left_dev)
        return [fr, fl], [nr, nl]

    def x_second(k, xs):
        arrived(xs[0])

        def fill_near(i, _):
            x_out[k, 1, i] = (acc(k, i, right) + x_mid[k, i].astype(f32)).astype(bf16)
            x_out[k, 1, 4 + i] = (acc(k, 4 + i, left) + x_mid[k, 4 + i].astype(f32)).astype(bf16)
            return 0

        lax.fori_loop(0, 4, fill_near, 0)
        return xs[1] + [
            push(k, x_out.at[k, 1, first], x_in.at[k, 0, first], 4, right_dev),
            push(k, x_out.at[k, 1, second], x_in.at[k, 1, second], 5, left_dev),
        ]

    def y_start(k, xs):
        arrived(xs)

        def total(i):
            return acc(k, i, x) + x_in[k, 0, i].astype(f32) + x_in[k, 1, i].astype(f32)

        def fill(i, _):
            y_out[k, i] = total(i).astype(bf16)
            return 0

        lax.fori_loop(0, 8, fill, 0)
        copies = [remote(y_out.at[k, ys[j]], y_in.at[k, j], y_send.at[k, j], y_recv.at[k, j], y_dev[j]) for j in range(7)]
        for copy in copies:
            copy.start()
        sent.extend(copies)
        y_own[k] = total(y)
        return copies

    def z_start(m, ycs):
        for p in range(2):
            arrived(ycs[p])
            v = y_own[p * 3 + m]
            for j in range(7):
                v = v + y_in[p * 3 + m, j].astype(f32)
            z_out[m, p] = v
        copy = remote(z_out.at[m, 1 - zlo], z_in.at[m], z_send.at[m], z_recv.at[m], pair_dev)
        copy.start()
        sent.append(copy)
        return copy

    def input_grad(n, _):
        at = pl.ds(pl.multiple_of(n * 256, 256), 256)
        v = jnp.zeros((ROWS, 256), f32)
        for p in range(2):
            for m in range(2):
                hi, lo = whi[p * 3 + m, at, :], wlo[p * 3 + m, at, :]
                v += dot(shi[p * 2 + m], hi, ((1,), (1,)))
                v += dot(shi[p * 2 + m], lo, ((1,), (1,)))
                v += dot(slo[p * 2 + m], hi, ((1,), (1,)))
        dxb[:, at] = v.astype(bf16)
        return 0

    returns = []

    def give(src, dst, n, lo, width):
        for i, k in enumerate((3, 1, 2)):
            at = (pl.ds(k * CAP, CAP), pl.ds(lo, width))
            copy = remote(src.at[at], dst.at[at], r_send.at[n, i], r_recv.at[n, i], come_dev[k - 1])
            copy.start()
            returns.append(copy)
        dst[pl.ds(0, CAP), lo:lo + width] = src[pl.ds(0, CAP), lo:lo + width]

    forward(0)
    turn(rcot, cot_t)
    c02 = weight_grad(0, 2, cot_t)
    c00 = weight_grad(0, 0, tok_t)
    forward(1)
    x02 = x_first(2, c02)
    lax.fori_loop(0, 4, input_grad, 0)
    give(dxb, back_ref, 0, 0, D // 2)
    dpb[...] = gprob[...].astype(bf16)
    give(dpb, backp_ref, 1, 0, EXTRA)
    x00 = x_first(0, c00)
    c01 = weight_grad(0, 1, tok_t)
    x02 = x_second(2, x02)
    lax.fori_loop(4, 8, input_grad, 0)
    give(dxb, back_ref, 2, D // 2, D // 2)
    x01 = x_first(1, c01)
    x00 = x_second(0, x00)
    c12 = weight_grad(1, 2, cot_t)
    c10 = weight_grad(1, 0, tok_t)
    x12 = x_first(5, c12)
    y02 = y_start(2, x02)
    x01 = x_second(1, x01)
    c11 = weight_grad(1, 1, tok_t)
    x10 = x_first(3, c10)
    y00 = y_start(0, x00)
    x12 = x_second(5, x12)
    x11 = x_first(4, c11)
    y01 = y_start(1, x01)
    x10 = x_second(3, x10)
    y12 = y_start(5, x12)
    x11 = x_second(4, x11)
    y10 = y_start(3, x10)
    z2 = z_start(2, (y02, y12))
    y11 = y_start(4, x11)
    z0 = z_start(0, (y00, y10))
    z1 = z_start(1, (y01, y11))
    arrived(returns)
    scale = 1.0 / math.sqrt(NX * NY * NZ * NC * 128)
    for m, copy in ((2, z2), (0, z0), (1, z1)):
        copy.wait_recv()
        out_ref[m] = (z_out[m, zlo] + z_in[m]) * scale
    for copy in tokens + sent + returns:
        copy.wait_send()


def layer(info, tokens, cots, packed, steps):
    vmem = pl.BlockSpec(memory_space=pltpu.VMEM)
    dma = pltpu.SemaphoreType.DMA
    V = pltpu.VMEM
    return pl.pallas_call(
        layer_kernel,
        out_shape=[
            jax.ShapeDtypeStruct((ROWS, D), bf16),
            jax.ShapeDtypeStruct((ROWS, EXTRA), bf16),
            jax.ShapeDtypeStruct((3, 64, FQ), f32),
        ],
        in_specs=[vmem] * 5,
        out_specs=[vmem] * 3,
        scratch_shapes=[
            V((ROWS, WIDE), bf16), V((ROWS, D), bf16), V((D, ROWS), bf16), V((D, ROWS), bf16),
            V((ROWS, WIDE), bf16), V((ROWS, D), bf16), V((12, D // 2, FQ), i32), V((2, 2, 8, FQ), f32),
            V((6, D, PAIR), bf16), V((6, D, PAIR), bf16),
            V((6, ROWS, PAIR), bf16), V((6, ROWS, PAIR), bf16), V((4, ROWS, PAIR), bf16), V((4, ROWS, PAIR), bf16),
            V((ROWS, D), bf16), V((ROWS, EXTRA), bf16), V((ROWS, EXTRA), f32),
            V((6, 32, 2, 64, FQ), f32), V((6, 32, 64, FQ), f32),
            V((6, 4, 8, 64, FQ), bf16), V((6, 2, 8, 64, FQ), bf16), V((6, 8, 64, FQ), bf16),
            V((6, 64, FQ), f32), V((6, 8, 64, FQ), bf16), V((6, 7, 64, FQ), bf16),
            V((3, 2, 64, FQ), f32), V((3, 64, FQ), f32),
            dma((2,)), dma((2,)), dma((3, 2)), dma((3, 2)), dma((2,)), dma((2,)), dma((2, 7)), dma((2, 7)), dma((2, 8)), dma((2, 8)),
            dma((4, 4)), dma((4, 4)), dma((4,)), dma((4,)), dma((3, 3)), dma((3, 3)), dma((6,)), dma((6,)), dma((6, 6)), dma((6, 6)),
            dma((6, 7)), dma((6, 7)), dma((3,)), dma((3,)), dma((3,)),
        ],
        compiler_params=pltpu.CompilerParams(
            collective_id=0, has_side_effects=True, vmem_limit_bytes=62 * 1024 * 1024
        ),
    )(info, tokens, cots, packed, steps)


def shards(tokens, cotangent, route, prob, w_gate, w_up, w_down):
    x, y, z, c = coords()
    odd = lax.rem(z, 2)
    turn = lax.rem(route[:, 0] - lax.div(z, 2) + HOT, HOT)
    slot = jnp.where(turn == 0, 0, jnp.where(turn == 1, 2 - odd, jnp.where(turn == 2, 3, 1 + odd)))
    onehot = (slot[:, None] == jnp.arange(HOT, dtype=jnp.int32)[None, :]).astype(f32)
    before = (jnp.arange(128)[:, None] > jnp.arange(128)[None, :]).astype(bf16)
    earlier = jnp.dot(before, onehot.astype(bf16), preferred_element_type=f32)
    rank = jnp.sum(earlier * onehot, axis=1).astype(jnp.int32)
    position = slot * CAP + rank
    ylo = lax.rem(y, NYL)
    starts = (((c * NX + x) * NYL + ylo) * 16, 512 + ((c * NYL + ylo) * NX + x) * 16)
    weights = (w_gate, w_up, w_down)
    tops = [jnp.maximum(jnp.max(jnp.abs(w[0]), axis=0), 1e-30) for w in weights]
    steps = jnp.stack([t * (1.0 / W_TOP) for t in tops])
    chunk = jnp.stack([
        jnp.stack([lax.dynamic_slice(w[0].reshape(2, D // 2, FQ), (0, start, 0), (2, 16, FQ)) for w in weights])
        for start in starts
    ])
    units = jnp.clip(jnp.round(chunk / steps[None, :, None, None, :]), -W_TOP, W_TOP).astype(i32)
    packed = units[:, :, 0] * 65536 + (units[:, :, 1] + 32768)
    info = jnp.stack([position.astype(f32), prob.astype(f32)] * 4)
    back, back_prob, mine = layer(info, tokens, cotangent, packed, jnp.pad(steps, ((0, 5), (0, 0))))
    taking = (position[:, None] == jnp.arange(ROWS, dtype=jnp.int32)[None, :]).astype(bf16)
    grad_input = jnp.dot(taking, back, preferred_element_type=f32).astype(bf16)
    grad_prob = jnp.dot(taking, back_prob, preferred_element_type=f32)[:, 0].astype(bf16)
    return (grad_input, grad_prob, mine[0][None], mine[1][None], mine[2][None])


def solution(mesh):
    rows = P(("dp", "expert"), None)
    placed = (rows, rows, rows, P(("dp", "expert")), P("expert", None, None), P("expert", None, None),
              P("expert", None, None))
    return jax.shard_map(
        shards,
        mesh=mesh,
        in_specs=placed,
        out_specs=(rows, P(("dp", "expert")), P("expert", "dp", None), P("expert", "dp", None),
                   P("expert", "dp", None)),
        check_vma=False,
    )
```

```python
import math

import jax
import jax.numpy as jnp
from jax import lax
from jax.experimental import pallas as pl
from jax.experimental.pallas import tpu as pltpu
from jax.sharding import PartitionSpec as P

D = 2048
HOT = 4
CAP = 48
FQ = 128
NX, NYL, NYH, NZ, NC = 4, 4, 2, 8, 2
NY = NYL * NYH
EXTRA = 128
ROWS = HOT * CAP
PAIR = 2 * FQ
WIDE = D + EXTRA
W_TOP = 32767.0
MESH = pl.DeviceIdType.MESH
f32, bf16, i32 = jnp.float32, jnp.bfloat16, jnp.int32


def coords():
    dp = lax.axis_index("dp")
    ex = lax.axis_index("expert")
    core = lax.rem(dp, NC)
    x = lax.rem(lax.div(dp, NC), NX)
    ylo = lax.div(dp, NC * NX)
    yhi = lax.rem(ex, NYH)
    z = lax.div(ex, NYH)
    return x, yhi * NYL + ylo, z, core


def device(x, y, z, core):
    return ((lax.rem(y, NYL) * NX + x) * NC + core, z * NYH + lax.div(y, NYL))


def slot_route(z, k):
    odd = lax.rem(z, 2)
    sign = 1 - 2 * odd
    to = sign * (k if k % 2 == 0 else -k)
    come = sign * -k
    return lax.rem(z + to + NZ, NZ), lax.rem(z + come + NZ, NZ)


def remote(src, dst, send, recv, dev):
    return pltpu.make_async_remote_copy(
        src_ref=src, dst_ref=dst, send_sem=send, recv_sem=recv, device_id=dev, device_id_type=MESH
    )


def enter(sources, count, meanwhile):
    barrier = pltpu.get_barrier_semaphore()
    for dev in sources:
        pl.semaphore_signal(barrier, inc=1, device_id=dev, device_id_type=MESH)
    meanwhile()
    pl.semaphore_wait(barrier, count)


def dot(a, b, dims):
    return lax.dot_general(a, b, (dims, ((), ())), preferred_element_type=f32)


def halves(v):
    hi = v.astype(bf16)
    return hi, (v - hi.astype(f32)).astype(bf16)


def layer_kernel(info_ref, tokens_ref, cots_ref, w_ref, s_ref, back_ref, backp_ref, out_ref,
                 tok_ref, cot_ref, tok_t, cot_t, rtok, rcot, wall, sall, whi, wlo, dhi, dlo, shi, slo, dxb, dpb, gprob,
                 g, c_in, x_out, x_in, x_mid, y_own, y_out, y_in, z_out, z_in, f_out, f_in, f_send, f_recv,
                 s_send, s_recv, t_send, t_recv, wz_send, wz_recv, wd_send, wd_recv, wy_send, wy_recv, wx_send, wx_recv, wc_send, wc_recv,
                 r_send, r_recv, c_send, c_recv, x_send, x_recv, y_send, y_recv, z_send, z_recv, loc):
    x, y, z, c = coords()
    ylo, yhi = lax.rem(y, NYL), lax.div(y, NYL)
    zlo = lax.rem(z, 2)
    zp = z + 1 - 2 * zlo
    right, left = lax.rem(x + 1, NX), lax.rem(x + NX - 1, NX)
    far = lax.rem(x + 2, NX)
    routes = [slot_route(z, k) for k in (1, 2, 3)]
    ys = [lax.rem(y + j, NY) for j in range(1, NY)]
    to_dev = [device(x, y, to, c) for to, _ in routes]
    come_dev = [device(x, y, come, c) for _, come in routes]
    pair_dev = device(x, y, zp, c)
    y_dev = [device(x, yy, z, c) for yy in ys]
    right_dev, left_dev, core_dev = device(right, y, z, c), device(left, y, z, c), device(x, y, z, 1 - c)
    def place():
        here = lax.broadcasted_iota(jnp.int32, (ROWS, 128), 0).astype(f32) == info_ref[0:1, :]
        prob = jnp.sum(jnp.where(here, info_ref[1:2, :], 0.0), axis=1, keepdims=True)
        placing = here.astype(f32).astype(bf16)
        tok_ref[:, :D] = dot(placing, tokens_ref[...], ((1,), (0,))).astype(bf16)
        tok_ref[:, D:] = jnp.broadcast_to(prob, (ROWS, EXTRA)).astype(bf16)
        cot_ref[...] = dot(placing, cots_ref[...], ((1,), (0,))).astype(bf16)

    enter([to_dev[0], to_dev[1], come_dev[1], to_dev[2], pair_dev] + y_dev + [right_dev, left_dev, core_dev], 15, place)

    up_dev, down_dev = y_dev[0], y_dev[6]

    def rows_at(start, n):
        return pl.ds(pl.multiple_of(start, 16), n)

    def y0_block(s, yy):
        return wall.at[pl.ds(s * 6 + lax.div(yy, NYL) * 3, 3), rows_at(((c * NX + x) * NYL + lax.rem(yy, NYL)) * 16, 16), :]

    def x0_block(s, xx, lo, n):
        return wall.at[pl.ds(s * 6 + lo, n), rows_at((c * NX + xx) * 64, 64), :]

    def x1_block(s, xx, lo, n):
        return wall.at[pl.ds(s * 6 + yhi * 3 + lo, n), rows_at(512 + ((c * NYL + ylo) * NX + xx) * 16, 16), :]

    def y1_block(s, yy, lo, n):
        return wall.at[pl.ds(s * 6 + lax.div(yy, NYL) * 3, 3), rows_at(512 + (c * NYL + lax.rem(yy, NYL)) * 64 + lo, n), :]

    mine = pl.ds((zlo * 2 + yhi) * 3, 3)
    places = [
        wall.at[mine, rows_at(((c * NX + x) * NYL + ylo) * 16, 16), :],
        wall.at[mine, rows_at(512 + ((c * NYL + ylo) * NX + x) * 16, 16), :],
    ]
    wz = [remote(w_ref.at[h], places[h], wz_send.at[h], wz_recv.at[h], pair_dev) for h in range(2)]
    sz = remote(s_ref, sall.at[zlo, yhi], s_send.at[0], s_recv.at[0], pair_dev)
    for copy in wz + [sz]:
        copy.start()
    tokens = []
    for j, (src, dst) in enumerate(((tok_ref, rtok), (cot_ref, rcot))):
        for i, k in enumerate((3, 1, 2)):
            at = pl.ds(k * CAP, CAP)
            copy = remote(src.at[at], dst.at[at], t_send.at[i, j], t_recv.at[i, j], to_dev[k - 1])
            copy.start()
            tokens.append(copy)
    locals_ = [
        pltpu.make_async_copy(w_ref.at[0], places[0], loc.at[0]),
        pltpu.make_async_copy(w_ref.at[1], places[1], loc.at[1]),
        pltpu.make_async_copy(s_ref, sall.at[zlo, yhi], loc.at[2]),
    ]
    for copy in locals_:
        copy.start()
    sent = []

    def start(src, send, recv, dev):
        copy = remote(src, src, send, recv, dev)
        copy.start()
        sent.append(copy)
        return copy

    def y_direct(i, s):
        return [start(y0_block(s, y), wd_send.at[i, j], wd_recv.at[i, j], y_dev[j]) for j in range(7)]

    def y_hop(i, s, d):
        back, ahead = lax.rem(y - d + NY, NY), lax.rem(y + d, NY)
        one, two = (y1_block(s, back, 0, 64), y1_block(s, ahead, 0, 64)) if d < 3 else (
            y1_block(s, back, 0, 32), y1_block(s, ahead, 32, 32))
        return [
            start(one, wy_send.at[i, 2 * d], wy_recv.at[i, 2 * d], up_dev),
            start(two, wy_send.at[i, 2 * d + 1], wy_recv.at[i, 2 * d + 1], down_dev),
        ]

    def x_hop(block, i, s, n):
        return [
            start(block(s, x, 0, n), wx_send.at[i, 0], wx_recv.at[i, 0], right_dev),
            start(block(s, x, 0, n), wx_send.at[i, 1], wx_recv.at[i, 1], left_dev),
        ]

    def x_relay(block, i, s, n):
        cut = n // 2
        return [
            start(block(s, left, 0, cut), wx_send.at[i, 2], wx_recv.at[i, 2], right_dev),
            start(block(s, right, cut, n - cut), wx_send.at[i, 3], wx_recv.at[i, 3], left_dev),
        ]

    def arrived(copies):
        for copy in copies:
            copy.wait_recv()

    def core_send(i, h, s):
        return start(wall.at[pl.ds(s * 6, 6), rows_at(h * 512 + c * 256, 256), :], wc_send.at[i], wc_recv.at[i], core_dev)

    sa, sb = zlo, 1 - zlo
    for copy in locals_:
        copy.wait()
    ya = y_direct(0, sa)
    xa = x_hop(x1_block, 2, sa, 3)
    wz[0].wait()
    yb = y_direct(1, sb)
    wz[1].wait()
    xb = x_hop(x1_block, 3, sb, 3)
    sz.wait()
    mates = sall.at[:, yhi]
    sy = start(mates, s_send.at[1], s_recv.at[1], y_dev[3])
    rtok[pl.ds(0, CAP), :] = tok_ref[pl.ds(0, CAP), :]
    rcot[pl.ds(0, CAP), :] = cot_ref[pl.ds(0, CAP), :]

    arrived(xa)
    xa = x_relay(x1_block, 2, sa, 3)
    arrived(xb)
    xb = x_relay(x1_block, 3, sb, 3)
    arrived(ya)
    x0a = x_hop(x0_block, 0, sa, 6)
    arrived(xa)
    y1a = y_hop(0, sa, 0)
    arrived(xb)
    y1b = y_hop(1, sb, 0)
    arrived(yb)
    x0b = x_hop(x0_block, 1, sb, 6)
    arrived(y1a)
    y1a = y_hop(0, sa, 1)
    arrived(y1b)
    y1b = y_hop(1, sb, 1)
    arrived(x0a)
    x0a = x_relay(x0_block, 0, sa, 6)
    arrived(y1a)
    y1a = y_hop(0, sa, 2)
    arrived(y1b)
    y1b = y_hop(1, sb, 2)
    arrived(x0b)
    x0b = x_relay(x0_block, 1, sb, 6)
    arrived(x0a)
    wcs = [core_send(0, 0, sa)]
    arrived(y1a)
    y1a = y_hop(0, sa, 3)
    arrived(y1b)
    y1b = y_hop(1, sb, 3)
    arrived(x0b)
    wcs.append(core_send(1, 0, sb))
    arrived(y1a)
    wcs.append(core_send(2, 1, sa))
    arrived(y1b)
    wcs.append(core_send(3, 1, sb))

    def unpack(base):
        def step(t, _):
            mp, at = lax.div(t, 2), pl.multiple_of(base + lax.rem(t, 2) * 128, 128)
            p, m = lax.div(mp, 3), lax.rem(mp, 3)
            for q in range(2):
                v = wall[(p * 2 + q) * 3 + m, pl.ds(at, 128), :]
                for begin, u in ((0, v >> 16), (D // 2, (v & 65535) - 32768)):
                    hi, lo = halves(u.astype(f32))
                    whi[mp, pl.ds(pl.multiple_of(begin + at, 128), 128), q * FQ:(q + 1) * FQ] = hi
                    wlo[mp, pl.ds(pl.multiple_of(begin + at, 128), 128), q * FQ:(q + 1) * FQ] = lo
            return 0

        lax.fori_loop(0, 12, step, 0)

    unpack(c * 256)
    unpack(512 + c * 256)
    arrived(tokens[:3])

    def turn(left_ref, out_t):
        def step(n, _):
            at = pl.ds(pl.multiple_of(n * 256, 256), 256)
            out_t[at, :] = jnp.transpose(left_ref[:, at])
            return 0

        lax.fori_loop(0, 8, step, 0)

    turn(rtok, tok_t)
    arrived(wcs)
    unpack((1 - c) * 256)
    unpack(512 + (1 - c) * 256)
    sy.wait_recv()

    gprob[...] = jnp.zeros_like(gprob)

    def forward(p):
        def pre(left, m):
            step = jnp.concatenate([sall[p, 0, pl.ds(m, 1), :], sall[p, 1, pl.ds(m, 1), :]], axis=1)
            both = dot(left, whi[p * 3 + m], ((1,), (0,))) + dot(left, wlo[p * 3 + m], ((1,), (0,)))
            return both * step, step

        toks = rtok[:, :D]
        gate_pre, gate_step = pre(toks, 0)
        up_pre, up_step = pre(toks, 1)
        if p == 0:
            arrived(tokens[3:])
        backward, _ = pre(rcot[...], 2)
        pr = rtok[:, D:].astype(f32)
        pr = jnp.concatenate([pr, pr], axis=1)
        sig = jax.nn.sigmoid(gate_pre)
        act = gate_pre * sig
        hidden = act * up_pre
        gprob[...] += jnp.broadcast_to(jnp.sum(hidden * backward, axis=1, keepdims=True), (ROWS, EXTRA))
        d_hidden = pr * backward
        d_up = d_hidden * act
        d_gate = d_hidden * up_pre * sig * (1.0 + gate_pre * (1.0 - sig))
        for m, v in enumerate((d_gate, d_up, pr * hidden)):
            hi, lo = halves(v)
            dhi[p * 3 + m] = hi
            dlo[p * 3 + m] = lo
        for m, v in enumerate((d_gate * gate_step, d_up * up_step)):
            hi, lo = halves(v)
            shi[p * 2 + m] = hi
            slo[p * 2 + m] = lo

    def weight_grad(p, m, left_ref):
        def step(n, _):
            lt = left_ref[pl.ds(pl.multiple_of(n * 256, 256), 256), :]
            v = dot(lt, dhi[p * 3 + m], ((1,), (0,))) + dot(lt, dlo[p * 3 + m], ((1,), (0,)))
            for q in range(2):
                for i in range(4):
                    g[p * 3 + m, q * 16 + n * 2 + i // 2, i % 2] = v[i * 64:(i + 1) * 64, q * FQ:(q + 1) * FQ]
            return 0

        lax.fori_loop(0, 8, step, 0)
        copy = remote(g.at[p * 3 + m, :, 1 - c], c_in.at[p * 3 + m], c_send.at[p * 3 + m], c_recv.at[p * 3 + m], core_dev)
        copy.start()
        sent.append(copy)
        return copy

    def acc(k, yy, xx):
        return g[k, yy * NX + xx, c] + c_in[k, yy * NX + xx]

    def push(k, src, dst, n, dev):
        copy = remote(src, dst, x_send.at[k, n], x_recv.at[k, n], dev)
        copy.start()
        sent.append(copy)
        return copy

    first, second = pl.ds(0, 4), pl.ds(4, 4)

    def x_first(k, came):
        if came is not None:
            came.wait_recv()

        def fill_far(i, _):
            x_out[k, 0, i] = acc(k, i, far).astype(bf16)
            return 0

        lax.fori_loop(0, 8, fill_far, 0)
        fr = push(k, x_out.at[k, 0, first], x_mid.at[k, first], 0, right_dev)
        fl = push(k, x_out.at[k, 0, second], x_mid.at[k, second], 1, left_dev)

        def fill_plain(i, _):
            x_out[k, 2, i] = acc(k, 4 + i, right).astype(bf16)
            x_out[k, 3, i] = acc(k, i, left).astype(bf16)
            return 0

        lax.fori_loop(0, 4, fill_plain, 0)
        nr = push(k, x_out.at[k, 2, first], x_in.at[k, 0, second], 2, right_dev)
        nl = push(k, x_out.at[k, 3, first], x_in.at[k, 1, first], 3, left_dev)
        return [fr, fl], [nr, nl]

    def x_second(k, xs):
        arrived(xs[0])

        def fill_near(i, _):
            x_out[k, 1, i] = (acc(k, i, right) + x_mid[k, i].astype(f32)).astype(bf16)
            x_out[k, 1, 4 + i] = (acc(k, 4 + i, left) + x_mid[k, 4 + i].astype(f32)).astype(bf16)
            return 0

        lax.fori_loop(0, 4, fill_near, 0)
        return xs[1] + [
            push(k, x_out.at[k, 1, first], x_in.at[k, 0, first], 4, right_dev),
            push(k, x_out.at[k, 1, second], x_in.at[k, 1, second], 5, left_dev),
        ]

    def y_start(k, xs):
        arrived(xs)

        def total(i):
            return acc(k, i, x) + x_in[k, 0, i].astype(f32) + x_in[k, 1, i].astype(f32)

        def fill(i, _):
            y_out[k, i] = total(i).astype(bf16)
            return 0

        lax.fori_loop(0, 8, fill, 0)
        copies = [remote(y_out.at[k, ys[j]], y_in.at[k, j], y_send.at[k, j], y_recv.at[k, j], y_dev[j]) for j in range(7)]
        for copy in copies:
            copy.start()
        sent.extend(copies)
        y_own[k] = total(y)
        return copies

    def z_start(m, ycs):
        for p in range(2):
            arrived(ycs[p])
            v = y_own[p * 3 + m]
            for j in range(7):
                v = v + y_in[p * 3 + m, j].astype(f32)
            z_out[m, p] = v
        copy = remote(z_out.at[m, 1 - zlo], z_in.at[m], z_send.at[m], z_recv.at[m], pair_dev)
        copy.start()
        sent.append(copy)
        return copy

    def input_grad(n, _):
        at = pl.ds(pl.multiple_of(n * 256, 256), 256)
        v = jnp.zeros((ROWS, 256), f32)
        for p in range(2):
            for m in range(2):
                hi, lo = whi[p * 3 + m, at, :], wlo[p * 3 + m, at, :]
                v += dot(shi[p * 2 + m], hi, ((1,), (1,)))
                v += dot(shi[p * 2 + m], lo, ((1,), (1,)))
                v += dot(slo[p * 2 + m], hi, ((1,), (1,)))
        dxb[:, at] = v.astype(bf16)
        return 0

    down, over_there = zlo * 3 + 2, (1 - zlo) * 3 + 2

    def z_first(*came):
        arrived(came)

        def fill(i, _):
            f_out[i] = (g[over_there, i, c] + c_in[over_there, i]).astype(bf16)
            return 0

        lax.fori_loop(0, 32, fill, 0)
        copy = remote(f_out, f_in, f_send, f_recv, pair_dev)
        copy.start()
        sent.append(copy)
        return copy

    def z_join(copy):
        copy.wait_recv()

        def fill(i, _):
            c_in[down, i] = c_in[down, i] + f_in[i].astype(f32)
            return 0

        lax.fori_loop(0, 32, fill, 0)

    returns = []

    def give(src, dst, n, lo, width):
        for i, k in enumerate((3, 1, 2)):
            at = (pl.ds(k * CAP, CAP), pl.ds(lo, width))
            copy = remote(src.at[at], dst.at[at], r_send.at[n, i], r_recv.at[n, i], come_dev[k - 1])
            copy.start()
            returns.append(copy)
        dst[pl.ds(0, CAP), lo:lo + width] = src[pl.ds(0, CAP), lo:lo + width]

    forward(0)
    turn(rcot, cot_t)
    c00 = weight_grad(0, 0, tok_t)
    c01 = weight_grad(0, 1, tok_t)
    forward(1)
    x00 = x_first(0, c00)
    c02 = weight_grad(0, 2, cot_t)
    c12 = weight_grad(1, 2, cot_t)
    x01 = x_first(1, c01)
    x00 = x_second(0, x00)
    over = z_first(c02, c12)
    c10 = weight_grad(1, 0, tok_t)
    x01 = x_second(1, x01)
    x10 = x_first(3, c10)
    y00 = y_start(0, x00)
    lax.fori_loop(0, 4, input_grad, 0)
    give(dxb, back_ref, 0, 0, D // 2)
    dpb[...] = gprob[...].astype(bf16)
    give(dpb, backp_ref, 1, 0, EXTRA)
    c11 = weight_grad(1, 1, tok_t)
    x10 = x_second(3, x10)
    y01 = y_start(1, x01)
    x11 = x_first(4, c11)
    z_join(over)
    x2 = x_first(down, None)
    lax.fori_loop(4, 8, input_grad, 0)
    give(dxb, back_ref, 2, D // 2, D // 2)
    x11 = x_second(4, x11)
    y10 = y_start(3, x10)
    x2 = x_second(down, x2)
    y11 = y_start(4, x11)
    z0 = z_start(0, (y00, y10))
    y2 = y_start(down, x2)
    z1 = z_start(1, (y01, y11))
    arrived(returns)
    scale = 1.0 / math.sqrt(NX * NY * NZ * NC * 128)
    for m, copy in ((0, z0), (1, z1)):
        copy.wait_recv()
        out_ref[m] = (z_out[m, zlo] + z_in[m]) * scale
    arrived(y2)
    v = y_own[down]
    for j in range(7):
        v = v + y_in[down, j].astype(f32)
    out_ref[2] = v * scale
    for copy in tokens + sent + returns:
        copy.wait_send()


def layer(info, tokens, cots, packed, steps):
    vmem = pl.BlockSpec(memory_space=pltpu.VMEM)
    dma = pltpu.SemaphoreType.DMA
    V = pltpu.VMEM
    return pl.pallas_call(
        layer_kernel,
        out_shape=[
            jax.ShapeDtypeStruct((ROWS, D), bf16),
            jax.ShapeDtypeStruct((ROWS, EXTRA), bf16),
            jax.ShapeDtypeStruct((3, 64, FQ), f32),
        ],
        in_specs=[vmem] * 5,
        out_specs=[vmem] * 3,
        scratch_shapes=[
            V((ROWS, WIDE), bf16), V((ROWS, D), bf16), V((D, ROWS), bf16), V((D, ROWS), bf16),
            V((ROWS, WIDE), bf16), V((ROWS, D), bf16), V((12, D // 2, FQ), i32), V((2, 2, 8, FQ), f32),
            V((6, D, PAIR), bf16), V((6, D, PAIR), bf16),
            V((6, ROWS, PAIR), bf16), V((6, ROWS, PAIR), bf16), V((4, ROWS, PAIR), bf16), V((4, ROWS, PAIR), bf16),
            V((ROWS, D), bf16), V((ROWS, EXTRA), bf16), V((ROWS, EXTRA), f32),
            V((6, 32, 2, 64, FQ), f32), V((6, 32, 64, FQ), f32),
            V((6, 4, 8, 64, FQ), bf16), V((6, 2, 8, 64, FQ), bf16), V((6, 8, 64, FQ), bf16),
            V((6, 64, FQ), f32), V((6, 8, 64, FQ), bf16), V((6, 7, 64, FQ), bf16),
            V((3, 2, 64, FQ), f32), V((3, 64, FQ), f32), V((32, 64, FQ), bf16), V((32, 64, FQ), bf16), dma, dma,
            dma((2,)), dma((2,)), dma((3, 2)), dma((3, 2)), dma((2,)), dma((2,)), dma((2, 7)), dma((2, 7)), dma((2, 8)), dma((2, 8)),
            dma((4, 4)), dma((4, 4)), dma((4,)), dma((4,)), dma((3, 3)), dma((3, 3)), dma((6,)), dma((6,)), dma((6, 6)), dma((6, 6)),
            dma((6, 7)), dma((6, 7)), dma((3,)), dma((3,)), dma((3,)),
        ],
        compiler_params=pltpu.CompilerParams(
            collective_id=0, has_side_effects=True, vmem_limit_bytes=62 * 1024 * 1024
        ),
    )(info, tokens, cots, packed, steps)


def shards(tokens, cotangent, route, prob, w_gate, w_up, w_down):
    x, y, z, c = coords()
    odd = lax.rem(z, 2)
    turn = lax.rem(route[:, 0] - lax.div(z, 2) + HOT, HOT)
    slot = jnp.where(turn == 0, 0, jnp.where(turn == 1, 2 - odd, jnp.where(turn == 2, 3, 1 + odd)))
    onehot = (slot[:, None] == jnp.arange(HOT, dtype=jnp.int32)[None, :]).astype(f32)
    before = (jnp.arange(128)[:, None] > jnp.arange(128)[None, :]).astype(bf16)
    earlier = jnp.dot(before, onehot.astype(bf16), preferred_element_type=f32)
    rank = jnp.sum(earlier * onehot, axis=1).astype(jnp.int32)
    position = slot * CAP + rank
    ylo = lax.rem(y, NYL)
    starts = (((c * NX + x) * NYL + ylo) * 16, 512 + ((c * NYL + ylo) * NX + x) * 16)
    weights = (w_gate, w_up, w_down)
    tops = [jnp.maximum(jnp.max(jnp.abs(w[0]), axis=0), 1e-30) for w in weights]
    steps = jnp.stack([t * (1.0 / W_TOP) for t in tops])
    chunk = jnp.stack([
        jnp.stack([lax.dynamic_slice(w[0].reshape(2, D // 2, FQ), (0, start, 0), (2, 16, FQ)) for w in weights])
        for start in starts
    ])
    units = jnp.clip(jnp.round(chunk / steps[None, :, None, None, :]), -W_TOP, W_TOP).astype(i32)
    packed = units[:, :, 0] * 65536 + (units[:, :, 1] + 32768)
    info = jnp.stack([position.astype(f32), prob.astype(f32)] * 4)
    back, back_prob, mine = layer(info, tokens, cotangent, packed, jnp.pad(steps, ((0, 5), (0, 0))))
    taking = (position[:, None] == jnp.arange(ROWS, dtype=jnp.int32)[None, :]).astype(bf16)
    grad_input = jnp.dot(taking, back, preferred_element_type=f32).astype(bf16)
    grad_prob = jnp.dot(taking, back_prob, preferred_element_type=f32)[:, 0].astype(bf16)
    return (grad_input, grad_prob, mine[0][None], mine[1][None], mine[2][None])


def solution(mesh):
    rows = P(("dp", "expert"), None)
    placed = (rows, rows, rows, P(("dp", "expert")), P("expert", None, None), P("expert", None, None),
              P("expert", None, None))
    return jax.shard_map(
        shards,
        mesh=mesh,
        in_specs=placed,
        out_specs=(rows, P(("dp", "expert")), P("expert", "dp", None), P("expert", "dp", None),
                   P("expert", "dp", None)),
        check_vma=False,
    )
```

```python
import math

import jax
import jax.numpy as jnp
from jax import lax
from jax.experimental import pallas as pl
from jax.experimental.pallas import tpu as pltpu
from jax.sharding import PartitionSpec as P

D = 2048
HOT = 4
CAP = 48
FQ = 128
NX, NYL, NYH, NZ, NC = 4, 4, 2, 8, 2
NY = NYL * NYH
EXTRA = 128
ROWS = HOT * CAP
PAIR = 2 * FQ
WIDE = D + EXTRA
W_TOP = 32767.0
MESH = pl.DeviceIdType.MESH
f32, bf16, i32 = jnp.float32, jnp.bfloat16, jnp.int32


def coords():
    dp = lax.axis_index("dp")
    ex = lax.axis_index("expert")
    core = lax.rem(dp, NC)
    x = lax.rem(lax.div(dp, NC), NX)
    ylo = lax.div(dp, NC * NX)
    yhi = lax.rem(ex, NYH)
    z = lax.div(ex, NYH)
    return x, yhi * NYL + ylo, z, core


def device(x, y, z, core):
    return ((lax.rem(y, NYL) * NX + x) * NC + core, z * NYH + lax.div(y, NYL))


def slot_route(z, k):
    odd = lax.rem(z, 2)
    sign = 1 - 2 * odd
    to = sign * (k if k % 2 == 0 else -k)
    come = sign * -k
    return lax.rem(z + to + NZ, NZ), lax.rem(z + come + NZ, NZ)


def remote(src, dst, send, recv, dev):
    return pltpu.make_async_remote_copy(
        src_ref=src, dst_ref=dst, send_sem=send, recv_sem=recv, device_id=dev, device_id_type=MESH
    )


def enter(sources, count, meanwhile):
    barrier = pltpu.get_barrier_semaphore()
    for dev in sources:
        pl.semaphore_signal(barrier, inc=1, device_id=dev, device_id_type=MESH)
    meanwhile()
    pl.semaphore_wait(barrier, count)


def dot(a, b, dims):
    return lax.dot_general(a, b, (dims, ((), ())), preferred_element_type=f32)


def halves(v):
    hi = v.astype(bf16)
    return hi, (v - hi.astype(f32)).astype(bf16)


def layer_kernel(info_ref, tokens_ref, cots_ref, w_ref, s_ref, back_ref, backp_ref, out_ref,
                 tok_ref, cot_ref, tok_t, cot_t, rtok, rcot, wall, sall, whi, wlo, dhi, dlo, shi, slo, dxb, dpb, gprob,
                 g, c_in, x_out, x_in, x_mid, y_own, y_out, y_in, z_out, z_in,
                 s_send, s_recv, t_send, t_recv, wz_send, wz_recv, wd_send, wd_recv, wy_send, wy_recv, wx_send, wx_recv, wc_send, wc_recv,
                 r_send, r_recv, c_send, c_recv, x_send, x_recv, y_send, y_recv, z_send, z_recv, loc):
    x, y, z, c = coords()
    ylo, yhi = lax.rem(y, NYL), lax.div(y, NYL)
    zlo = lax.rem(z, 2)
    zp = z + 1 - 2 * zlo
    right, left = lax.rem(x + 1, NX), lax.rem(x + NX - 1, NX)
    far = lax.rem(x + 2, NX)
    routes = [slot_route(z, k) for k in (1, 2, 3)]
    ys = [lax.rem(y + j, NY) for j in range(1, NY)]
    to_dev = [device(x, y, to, c) for to, _ in routes]
    come_dev = [device(x, y, come, c) for _, come in routes]
    pair_dev = device(x, y, zp, c)
    y_dev = [device(x, yy, z, c) for yy in ys]
    right_dev, left_dev, core_dev = device(right, y, z, c), device(left, y, z, c), device(x, y, z, 1 - c)
    def place():
        here = lax.broadcasted_iota(jnp.int32, (ROWS, 128), 0).astype(f32) == info_ref[0:1, :]
        prob = jnp.sum(jnp.where(here, info_ref[1:2, :], 0.0), axis=1, keepdims=True)
        placing = here.astype(f32).astype(bf16)
        tok_ref[:, :D] = dot(placing, tokens_ref[...], ((1,), (0,))).astype(bf16)
        tok_ref[:, D:] = jnp.broadcast_to(prob, (ROWS, EXTRA)).astype(bf16)
        cot_ref[...] = dot(placing, cots_ref[...], ((1,), (0,))).astype(bf16)

    enter([to_dev[0], to_dev[1], come_dev[1], to_dev[2], pair_dev] + y_dev + [right_dev, left_dev, core_dev], 15, place)

    up_dev, down_dev = y_dev[0], y_dev[6]

    def rows_at(start, n):
        return pl.ds(pl.multiple_of(start, 16), n)

    def y0_block(s, yy):
        return wall.at[pl.ds(s * 6 + lax.div(yy, NYL) * 3, 3), rows_at(((c * NX + x) * NYL + lax.rem(yy, NYL)) * 16, 16), :]

    def x0_block(s, xx, lo, n):
        return wall.at[pl.ds(s * 6 + lo, n), rows_at((c * NX + xx) * 64, 64), :]

    def x1_block(s, xx, lo, n):
        return wall.at[pl.ds(s * 6 + yhi * 3 + lo, n), rows_at(512 + ((c * NYL + ylo) * NX + xx) * 16, 16), :]

    def y1_block(s, yy, lo, n):
        return wall.at[pl.ds(s * 6 + lax.div(yy, NYL) * 3, 3), rows_at(512 + (c * NYL + lax.rem(yy, NYL)) * 64 + lo, n), :]

    mine = pl.ds((zlo * 2 + yhi) * 3, 3)
    places = [
        wall.at[mine, rows_at(((c * NX + x) * NYL + ylo) * 16, 16), :],
        wall.at[mine, rows_at(512 + ((c * NYL + ylo) * NX + x) * 16, 16), :],
    ]
    wz = [remote(w_ref.at[h], places[h], wz_send.at[h], wz_recv.at[h], pair_dev) for h in range(2)]
    sz = remote(s_ref, sall.at[zlo, yhi], s_send.at[0], s_recv.at[0], pair_dev)
    for copy in wz + [sz]:
        copy.start()
    tokens = []
    for j, (src, dst) in enumerate(((tok_ref, rtok), (cot_ref, rcot))):
        for i, k in enumerate((3, 1, 2)):
            at = pl.ds(k * CAP, CAP)
            copy = remote(src.at[at], dst.at[at], t_send.at[i, j], t_recv.at[i, j], to_dev[k - 1])
            copy.start()
            tokens.append(copy)
    locals_ = [
        pltpu.make_async_copy(w_ref.at[0], places[0], loc.at[0]),
        pltpu.make_async_copy(w_ref.at[1], places[1], loc.at[1]),
        pltpu.make_async_copy(s_ref, sall.at[zlo, yhi], loc.at[2]),
    ]
    for copy in locals_:
        copy.start()
    sent = []

    def start(src, send, recv, dev):
        copy = remote(src, src, send, recv, dev)
        copy.start()
        sent.append(copy)
        return copy

    def y_direct(i, s):
        return [start(y0_block(s, y), wd_send.at[i, j], wd_recv.at[i, j], y_dev[j]) for j in range(7)]

    def y_hop(i, s, d):
        back, ahead = lax.rem(y - d + NY, NY), lax.rem(y + d, NY)
        one, two = (y1_block(s, back, 0, 64), y1_block(s, ahead, 0, 64)) if d < 3 else (
            y1_block(s, back, 0, 32), y1_block(s, ahead, 32, 32))
        return [
            start(one, wy_send.at[i, 2 * d], wy_recv.at[i, 2 * d], up_dev),
            start(two, wy_send.at[i, 2 * d + 1], wy_recv.at[i, 2 * d + 1], down_dev),
        ]

    def x_hop(block, i, s, n):
        return [
            start(block(s, x, 0, n), wx_send.at[i, 0], wx_recv.at[i, 0], right_dev),
            start(block(s, x, 0, n), wx_send.at[i, 1], wx_recv.at[i, 1], left_dev),
        ]

    def x_relay(block, i, s, n):
        cut = n // 2
        return [
            start(block(s, left, 0, cut), wx_send.at[i, 2], wx_recv.at[i, 2], right_dev),
            start(block(s, right, cut, n - cut), wx_send.at[i, 3], wx_recv.at[i, 3], left_dev),
        ]

    def arrived(copies):
        for copy in copies:
            copy.wait_recv()

    def core_send(i, h, s):
        return start(wall.at[pl.ds(s * 6, 6), rows_at(h * 512 + c * 256, 256), :], wc_send.at[i], wc_recv.at[i], core_dev)

    sa, sb = zlo, 1 - zlo
    for copy in locals_:
        copy.wait()
    ya = y_direct(0, sa)
    xa = x_hop(x1_block, 2, sa, 3)
    wz[0].wait()
    yb = y_direct(1, sb)
    wz[1].wait()
    xb = x_hop(x1_block, 3, sb, 3)
    sz.wait()
    mates = sall.at[:, yhi]
    sy = start(mates, s_send.at[1], s_recv.at[1], y_dev[3])
    rtok[pl.ds(0, CAP), :] = tok_ref[pl.ds(0, CAP), :]
    rcot[pl.ds(0, CAP), :] = cot_ref[pl.ds(0, CAP), :]

    arrived(xa)
    xa = x_relay(x1_block, 2, sa, 3)
    arrived(xb)
    xb = x_relay(x1_block, 3, sb, 3)
    arrived(ya)
    x0a = x_hop(x0_block, 0, sa, 6)
    arrived(xa)
    y1a = y_hop(0, sa, 0)
    arrived(xb)
    y1b = y_hop(1, sb, 0)
    arrived(yb)
    x0b = x_hop(x0_block, 1, sb, 6)
    arrived(y1a)
    y1a = y_hop(0, sa, 1)
    arrived(y1b)
    y1b = y_hop(1, sb, 1)
    arrived(x0a)
    x0a = x_relay(x0_block, 0, sa, 6)
    arrived(y1a)
    y1a = y_hop(0, sa, 2)
    arrived(y1b)
    y1b = y_hop(1, sb, 2)
    arrived(x0b)
    x0b = x_relay(x0_block, 1, sb, 6)
    arrived(x0a)
    wcs = [core_send(0, 0, sa)]
    arrived(y1a)
    y1a = y_hop(0, sa, 3)
    arrived(y1b)
    y1b = y_hop(1, sb, 3)
    arrived(x0b)
    wcs.append(core_send(1, 0, sb))
    arrived(y1a)
    wcs.append(core_send(2, 1, sa))
    arrived(y1b)
    wcs.append(core_send(3, 1, sb))

    def unpack(base):
        def step(t, _):
            mp, at = lax.div(t, 2), pl.multiple_of(base + lax.rem(t, 2) * 128, 128)
            p, m = lax.div(mp, 3), lax.rem(mp, 3)
            for q in range(2):
                v = wall[(p * 2 + q) * 3 + m, pl.ds(at, 128), :]
                for begin, u in ((0, v >> 16), (D // 2, (v & 65535) - 32768)):
                    hi, lo = halves(u.astype(f32))
                    whi[mp, pl.ds(pl.multiple_of(begin + at, 128), 128), q * FQ:(q + 1) * FQ] = hi
                    wlo[mp, pl.ds(pl.multiple_of(begin + at, 128), 128), q * FQ:(q + 1) * FQ] = lo
            return 0

        lax.fori_loop(0, 12, step, 0)

    unpack(c * 256)
    unpack(512 + c * 256)
    arrived(tokens[:3])

    def turn(left_ref, out_t):
        def step(n, _):
            at = pl.ds(pl.multiple_of(n * 256, 256), 256)
            out_t[at, :] = jnp.transpose(left_ref[:, at])
            return 0

        lax.fori_loop(0, 8, step, 0)

    turn(rtok, tok_t)
    arrived(wcs)
    unpack((1 - c) * 256)
    unpack(512 + (1 - c) * 256)
    sy.wait_recv()

    gprob[...] = jnp.zeros_like(gprob)

    def forward(p):
        def pre(left, m):
            step = jnp.concatenate([sall[p, 0, pl.ds(m, 1), :], sall[p, 1, pl.ds(m, 1), :]], axis=1)
            both = dot(left, whi[p * 3 + m], ((1,), (0,))) + dot(left, wlo[p * 3 + m], ((1,), (0,)))
            return both * step, step

        toks = rtok[:, :D]
        gate_pre, gate_step = pre(toks, 0)
        up_pre, up_step = pre(toks, 1)
        if p == 0:
            arrived(tokens[3:])
        backward, _ = pre(rcot[...], 2)
        pr = rtok[:, D:].astype(f32)
        pr = jnp.concatenate([pr, pr], axis=1)
        sig = jax.nn.sigmoid(gate_pre)
        act = gate_pre * sig
        hidden = act * up_pre
        gprob[...] += jnp.broadcast_to(jnp.sum(hidden * backward, axis=1, keepdims=True), (ROWS, EXTRA))
        d_hidden = pr * backward
        d_up = d_hidden * act
        d_gate = d_hidden * up_pre * sig * (1.0 + gate_pre * (1.0 - sig))
        for m, v in enumerate((d_gate, d_up, pr * hidden)):
            hi, lo = halves(v)
            dhi[p * 3 + m] = hi
            dlo[p * 3 + m] = lo
        for m, v in enumerate((d_gate * gate_step, d_up * up_step)):
            hi, lo = halves(v)
            shi[p * 2 + m] = hi
            slo[p * 2 + m] = lo

    def weight_grad(p, m, left_ref):
        def step(n, _):
            lt = left_ref[pl.ds(pl.multiple_of(n * 256, 256), 256), :]
            v = dot(lt, dhi[p * 3 + m], ((1,), (0,))) + dot(lt, dlo[p * 3 + m], ((1,), (0,)))
            for q in range(2):
                for i in range(4):
                    g[p * 3 + m, q * 16 + n * 2 + i // 2, i % 2] = v[i * 64:(i + 1) * 64, q * FQ:(q + 1) * FQ]
            return 0

        lax.fori_loop(0, 8, step, 0)
        copy = remote(g.at[p * 3 + m, :, 1 - c], c_in.at[p * 3 + m], c_send.at[p * 3 + m], c_recv.at[p * 3 + m], core_dev)
        copy.start()
        sent.append(copy)
        return copy

    def acc(k, yy, xx):
        return g[k, yy * NX + xx, c] + c_in[k, yy * NX + xx]

    def push(k, src, dst, n, dev):
        copy = remote(src, dst, x_send.at[k, n], x_recv.at[k, n], dev)
        copy.start()
        sent.append(copy)
        return copy

    first, second = pl.ds(0, 4), pl.ds(4, 4)

    def x_first(k, came):
        came.wait_recv()

        def fill_far(i, _):
            x_out[k, 0, i] = acc(k, i, far).astype(bf16)
            return 0

        lax.fori_loop(0, 8, fill_far, 0)
        fr = push(k, x_out.at[k, 0, first], x_mid.at[k, first], 0, right_dev)
        fl = push(k, x_out.at[k, 0, second], x_mid.at[k, second], 1, left_dev)

        def fill_plain(i, _):
            x_out[k, 2, i] = acc(k, 4 + i, right).astype(bf16)
            x_out[k, 3, i] = acc(k, i, left).astype(bf16)
            return 0

        lax.fori_loop(0, 4, fill_plain, 0)
        nr = push(k, x_out.at[k, 2, first], x_in.at[k, 0, second], 2, right_dev)
        nl = push(k, x_out.at[k, 3, first], x_in.at[k, 1, first], 3, left_dev)
        return [fr, fl], [nr, nl]

    def x_second(k, xs):
        arrived(xs[0])

        def fill_near(i, _):
            x_out[k, 1, i] = (acc(k, i, right) + x_mid[k, i].astype(f32)).astype(bf16)
            x_out[k, 1, 4 + i] = (acc(k, 4 + i, left) + x_mid[k, 4 + i].astype(f32)).astype(bf16)
            return 0

        lax.fori_loop(0, 4, fill_near, 0)
        return xs[1] + [
            push(k, x_out.at[k, 1, first], x_in.at[k, 0, first], 4, right_dev),
            push(k, x_out.at[k, 1, second], x_in.at[k, 1, second], 5, left_dev),
        ]

    def y_start(k, xs):
        arrived(xs)

        def total(i):
            return acc(k, i, x) + x_in[k, 0, i].astype(f32) + x_in[k, 1, i].astype(f32)

        def fill(i, _):
            y_out[k, i] = total(i).astype(bf16)
            return 0

        lax.fori_loop(0, 8, fill, 0)
        copies = [remote(y_out.at[k, ys[j]], y_in.at[k, j], y_send.at[k, j], y_recv.at[k, j], y_dev[j]) for j in range(7)]
        for copy in copies:
            copy.start()
        sent.extend(copies)
        y_own[k] = total(y)
        return copies

    def z_start(m, ycs):
        for p in range(2):
            arrived(ycs[p])
            v = y_own[p * 3 + m]
            for j in range(7):
                v = v + y_in[p * 3 + m, j].astype(f32)
            z_out[m, p] = v
        copy = remote(z_out.at[m, 1 - zlo], z_in.at[m], z_send.at[m], z_recv.at[m], pair_dev)
        copy.start()
        sent.append(copy)
        return copy

    def input_grad(n, _):
        at = pl.ds(pl.multiple_of(n * 256, 256), 256)
        v = jnp.zeros((ROWS, 256), f32)
        for p in range(2):
            for m in range(2):
                hi, lo = whi[p * 3 + m, at, :], wlo[p * 3 + m, at, :]
                v += dot(shi[p * 2 + m], hi, ((1,), (1,)))
                v += dot(shi[p * 2 + m], lo, ((1,), (1,)))
                v += dot(slo[p * 2 + m], hi, ((1,), (1,)))
        dxb[:, at] = v.astype(bf16)
        return 0

    returns = []

    def give(src, dst, n, lo, width):
        for i, k in enumerate((3, 1, 2)):
            at = (pl.ds(k * CAP, CAP), pl.ds(lo, width))
            copy = remote(src.at[at], dst.at[at], r_send.at[n, i], r_recv.at[n, i], come_dev[k - 1])
            copy.start()
            returns.append(copy)
        dst[pl.ds(0, CAP), lo:lo + width] = src[pl.ds(0, CAP), lo:lo + width]

    forward(0)
    turn(rcot, cot_t)
    c02 = weight_grad(0, 2, cot_t)
    c00 = weight_grad(0, 0, tok_t)
    x02 = x_first(2, c02)
    forward(1)
    c01 = weight_grad(0, 1, tok_t)
    x00 = x_first(0, c00)
    x02 = x_second(2, x02)
    c12 = weight_grad(1, 2, cot_t)
    x01 = x_first(1, c01)
    lax.fori_loop(0, 4, input_grad, 0)
    give(dxb, back_ref, 0, 0, D // 2)
    dpb[...] = gprob[...].astype(bf16)
    give(dpb, backp_ref, 1, 0, EXTRA)
    x00 = x_second(0, x00)
    c10 = weight_grad(1, 0, tok_t)
    x12 = x_first(5, c12)
    y02 = y_start(2, x02)
    x01 = x_second(1, x01)
    lax.fori_loop(4, 8, input_grad, 0)
    give(dxb, back_ref, 2, D // 2, D // 2)
    c11 = weight_grad(1, 1, tok_t)
    x10 = x_first(3, c10)
    y00 = y_start(0, x00)
    x12 = x_second(5, x12)
    x11 = x_first(4, c11)
    y01 = y_start(1, x01)
    x10 = x_second(3, x10)
    y12 = y_start(5, x12)
    x11 = x_second(4, x11)
    y10 = y_start(3, x10)
    z2 = z_start(2, (y02, y12))
    y11 = y_start(4, x11)
    z0 = z_start(0, (y00, y10))
    z1 = z_start(1, (y01, y11))
    arrived(returns)
    scale = 1.0 / math.sqrt(NX * NY * NZ * NC * 128)
    for m, copy in ((2, z2), (0, z0), (1, z1)):
        copy.wait_recv()
        out_ref[m] = (z_out[m, zlo] + z_in[m]) * scale
    for copy in tokens + sent + returns:
        copy.wait_send()


def layer(info, tokens, cots, packed, steps):
    vmem = pl.BlockSpec(memory_space=pltpu.VMEM)
    dma = pltpu.SemaphoreType.DMA
    V = pltpu.VMEM
    return pl.pallas_call(
        layer_kernel,
        out_shape=[
            jax.ShapeDtypeStruct((ROWS, D), bf16),
            jax.ShapeDtypeStruct((ROWS, EXTRA), bf16),
            jax.ShapeDtypeStruct((3, 64, FQ), f32),
        ],
        in_specs=[vmem] * 5,
        out_specs=[vmem] * 3,
        scratch_shapes=[
            V((ROWS, WIDE), bf16), V((ROWS, D), bf16), V((D, ROWS), bf16), V((D, ROWS), bf16),
            V((ROWS, WIDE), bf16), V((ROWS, D), bf16), V((12, D // 2, FQ), i32), V((2, 2, 8, FQ), f32),
            V((6, D, PAIR), bf16), V((6, D, PAIR), bf16),
            V((6, ROWS, PAIR), bf16), V((6, ROWS, PAIR), bf16), V((4, ROWS, PAIR), bf16), V((4, ROWS, PAIR), bf16),
            V((ROWS, D), bf16), V((ROWS, EXTRA), bf16), V((ROWS, EXTRA), f32),
            V((6, 32, 2, 64, FQ), f32), V((6, 32, 64, FQ), f32),
            V((6, 4, 8, 64, FQ), bf16), V((6, 2, 8, 64, FQ), bf16), V((6, 8, 64, FQ), bf16),
            V((6, 64, FQ), f32), V((6, 8, 64, FQ), bf16), V((6, 7, 64, FQ), bf16),
            V((3, 2, 64, FQ), f32), V((3, 64, FQ), f32),
            dma((2,)), dma((2,)), dma((3, 2)), dma((3, 2)), dma((2,)), dma((2,)), dma((2, 7)), dma((2, 7)), dma((2, 8)), dma((2, 8)),
            dma((4, 4)), dma((4, 4)), dma((4,)), dma((4,)), dma((3, 3)), dma((3, 3)), dma((6,)), dma((6,)), dma((6, 6)), dma((6, 6)),
            dma((6, 7)), dma((6, 7)), dma((3,)), dma((3,)), dma((3,)),
        ],
        compiler_params=pltpu.CompilerParams(
            collective_id=0, has_side_effects=True, vmem_limit_bytes=62 * 1024 * 1024
        ),
    )(info, tokens, cots, packed, steps)


def shards(tokens, cotangent, route, prob, w_gate, w_up, w_down):
    x, y, z, c = coords()
    odd = lax.rem(z, 2)
    turn = lax.rem(route[:, 0] - lax.div(z, 2) + HOT, HOT)
    slot = jnp.where(turn == 0, 0, jnp.where(turn == 1, 2 - odd, jnp.where(turn == 2, 3, 1 + odd)))
    onehot = (slot[:, None] == jnp.arange(HOT, dtype=jnp.int32)[None, :]).astype(f32)
    before = (jnp.arange(128)[:, None] > jnp.arange(128)[None, :]).astype(bf16)
    earlier = jnp.dot(before, onehot.astype(bf16), preferred_element_type=f32)
    rank = jnp.sum(earlier * onehot, axis=1).astype(jnp.int32)
    position = slot * CAP + rank
    ylo = lax.rem(y, NYL)
    starts = (((c * NX + x) * NYL + ylo) * 16, 512 + ((c * NYL + ylo) * NX + x) * 16)
    weights = (w_gate, w_up, w_down)
    tops = [jnp.maximum(jnp.max(jnp.abs(w[0]), axis=0), 1e-30) for w in weights]
    steps = jnp.stack([t * (1.0 / W_TOP) for t in tops])
    chunk = jnp.stack([
        jnp.stack([lax.dynamic_slice(w[0].reshape(2, D // 2, FQ), (0, start, 0), (2, 16, FQ)) for w in weights])
        for start in starts
    ])
    units = jnp.clip(jnp.round(chunk / steps[None, :, None, None, :]), -W_TOP, W_TOP).astype(i32)
    packed = units[:, :, 0] * 65536 + (units[:, :, 1] + 32768)
    info = jnp.stack([position.astype(f32), prob.astype(f32)] * 4)
    back, back_prob, mine = layer(info, tokens, cotangent, packed, jnp.pad(steps, ((0, 5), (0, 0))))
    taking = (position[:, None] == jnp.arange(ROWS, dtype=jnp.int32)[None, :]).astype(bf16)
    grad_input = jnp.dot(taking, back, preferred_element_type=f32).astype(bf16)
    grad_prob = jnp.dot(taking, back_prob, preferred_element_type=f32)[:, 0].astype(bf16)
    return (grad_input, grad_prob, mine[0][None], mine[1][None], mine[2][None])


def solution(mesh):
    rows = P(("dp", "expert"), None)
    placed = (rows, rows, rows, P(("dp", "expert")), P("expert", None, None), P("expert", None, None),
              P("expert", None, None))
    return jax.shard_map(
        shards,
        mesh=mesh,
        in_specs=placed,
        out_specs=(rows, P(("dp", "expert")), P("expert", "dp", None), P("expert", "dp", None),
                   P("expert", "dp", None)),
        check_vma=False,
    )
```
